256 devices in a mesh: facet: 16 (over x, y), span: 16 (over z, core).
Axes of the slice: x: 4, y: 4, z: 8, core: 2. Of those that a mesh axis runs over, the one named last changes fastest.
Arguments:
- visibilities: bfloat16 [16, 512, 2, 1024], P('span', 'facet'), may hold values from -6 to 6
- coordinates: bfloat16 [16, 512, 2, 1024], P('span', 'facet'), may hold values from 4 to 124
- phases: float32 [16, 512, 1024], P('span', 'facet'), may hold values from -3.140625 to 3.140625
- sub_index: int32 [16, 512], replicated, may hold values from 0 to 4095, as said below
Outputs:
- dirty: float32 [8192, 8192], P(('facet', 'span'))
The draws below stay inside these ranges and needn't reach their ends.
Inputs may be any that keep to these rules, and one draw needn't show every extreme that they name: `sub_index`: within one span (one row) all 512 subgrid indices differ. A grid block is the set of subgrids with rows f * 4 to (f + 1) * 4 - 1 and columns j * 4 to (j + 1) * 4 - 1 for f < 16, j < 16; at most 4 indices of one row fall in one grid block, and in every row some grid block holds exactly 4 of them.
All inputs are finite; a program needn't handle non-finite values.
Results may differ from the reference program's by a relative error of at most 0.005.
Values may be sent and summed in bfloat16 or wider, within the bound.
No kernel may reach another device: no remote copies, remote signals or barrier semaphores. Data moves between devices by JAX's collectives and lax.ppermute only.
A program may use at most 64 MiB of HBM per device.

```python
import jax
import jax.numpy as jnp
from jax import lax

N = 8192
P_SIZE = 128
K = 1024
BLK_DEV = 32
CAP = 4
SIDE = 64
SPANS = 16
BLK_C = 512
BAND_SUB = 4
COL_SUB = 4
GBLOCKS = 256


def draw_sub_index(key, part):
    target_locations = GBLOCKS * CAP
    slots_block = BAND_SUB * COL_SUB
    count_of_bands = GBLOCKS // SPANS

    def one_span(span_key):
        sorting_keys = jax.random.split(span_key, 4)
        position = jnp.arange(target_locations, dtype=jnp.int32)
        owning_block = position // CAP
        band_of = owning_block // SPANS
        separation_length = jnp.abs(2 * band_of + 1 - count_of_bands)
        extra_reward = 3072 * (count_of_bands - separation_length) // count_of_bands
        compelled_choice = jax.random.randint(sorting_keys[0], (), 0, GBLOCKS)
        placement_merit = jax.random.randint(sorting_keys[1], (target_locations,), 0, 4096) + extra_reward + 16384 * (owning_block == compelled_choice).astype(jnp.int32)
        distinct = placement_merit * target_locations + position
        order = jnp.argsort(-distinct)
        chosen = jax.random.permutation(sorting_keys[2], order[:BLK_C])
        offset = jax.random.randint(sorting_keys[3], (GBLOCKS,), 0, slots_block)
        block_of = chosen // CAP
        local_slot = (chosen % CAP + offset[block_of]) % slots_block
        sub_row = block_of // SPANS * BAND_SUB + local_slot // COL_SUB
        sub_col = block_of % SPANS * COL_SUB + local_slot % COL_SUB
        return (sub_row * SIDE + sub_col).astype(jnp.int32)
    return jax.vmap(one_span)(jax.random.split(key, SPANS))


def shard_levels(key, dims, pieces, low, top_value):
    level = 1.0
    for axis_at, blocks in pieces:
        heights = jax.random.uniform(jax.random.fold_in(jax.random.fold_in(key, 6), axis_at), (blocks,), jnp.float32, low / len(pieces), top_value / len(pieces))
        level = level * jnp.repeat(jnp.exp(heights), dims[axis_at] // blocks).reshape((-1,) + (1,) * (len(dims) - 1 - axis_at))
    return level


def gaussian(rng, extent, scale, limit, cuts=(), kind=jnp.bfloat16):
    entries = scale * jax.random.normal(rng, extent, jnp.float32)
    if cuts:
        entries = entries * shard_levels(rng, extent, cuts, -0.22, 0.18)
    return jnp.clip(entries, -limit, limit).astype(kind)


def setup_inputs(seed: int = 0) -> dict:
    arg_keys = jax.random.split(jax.random.key(seed), 5)
    visibilities = gaussian(arg_keys[0], (SPANS, BLK_C, 2, K), 1.0, 6.0, ((0, 16), (1, 16)))
    coordinates = jnp.clip(4.0 + 120.0 * jax.random.uniform(arg_keys[1], (SPANS, BLK_C, 2, K), jnp.float32) ** shard_levels(arg_keys[1], (SPANS, BLK_C, 2, K), ((0, 16), (1, 16)), -0.2, 0.2), 4.0, 124.0).astype(jnp.bfloat16)
    phases = jnp.clip(jax.random.uniform(arg_keys[2], (SPANS, BLK_C, K), jnp.float32, -3.140625, 3.140625), -3.140625, 3.140625)
    sub_index = draw_sub_index(jax.random.fold_in(arg_keys[4], 71), 0)
    return {"visibilities": visibilities, "coordinates": coordinates, "phases": phases, "sub_index": sub_index}


spread = 0.75


def rotate(visibilities, phases):
    vis_float = visibilities.astype(jnp.float32)
    cosine = jnp.cos(phases)
    sine = jnp.sin(phases)
    real_part = vis_float[..., 0, :]
    imag_part = vis_float[..., 1, :]
    stacked = jnp.stack([real_part * cosine - imag_part * sine, real_part * sine + imag_part * cosine], axis=-2)
    return stacked.astype(jnp.bfloat16)


def kernel_rows(positions, cell_index):
    gap_size = cell_index - positions[..., None]
    return jnp.exp(-(gap_size * gap_size) / (2.0 * spread * spread))


def subgrids_of(vis_items, coord_items):
    cell_index = jnp.arange(P_SIZE, dtype=jnp.float32)
    coord_vals = coord_items.astype(jnp.float32)
    row_kernel = kernel_rows(coord_vals[:, 0, :], cell_index)
    col_kernel = kernel_rows(coord_vals[:, 1, :], cell_index).astype(jnp.bfloat16)
    weighted = (vis_items.astype(jnp.float32)[:, :, :, None] * row_kernel[:, None, :, :]).astype(jnp.bfloat16)
    weighted, col_kernel = lax.optimization_barrier((weighted, col_kernel))
    result = jnp.einsum("ezkp,ekq->ezpq", weighted.astype(jnp.float32), col_kernel.astype(jnp.float32), precision=lax.Precision.HIGHEST)
    return result.astype(jnp.bfloat16)


def group_subgrids(group_inputs):
    return subgrids_of(group_inputs[0], group_inputs[1])


def reference(visibilities, coordinates, phases, sub_index):
    rotated = rotate(visibilities, phases)
    side_count = N // P_SIZE
    group_count = BLK_C // BLK_DEV

    def add_span(slot_sums, inputs):
        vis_rows, coord_rows, index_row = inputs
        grouped = lax.map(group_subgrids, (vis_rows.reshape(group_count, BLK_DEV, 2, K), coord_rows.reshape(group_count, BLK_DEV, 2, K)))
        grouped = lax.optimization_barrier(grouped)
        block_subs = grouped.reshape(BLK_C, 2, P_SIZE, P_SIZE).astype(jnp.float32)
        return slot_sums.at[index_row].add(block_subs), None

    initial = jnp.zeros((side_count * side_count, 2, P_SIZE, P_SIZE), jnp.float32)
    slot_sums, unused = lax.scan(add_span, initial, (rotated, coordinates, sub_index))
    grid = slot_sums.reshape(side_count, side_count, 2, P_SIZE, P_SIZE).transpose(2, 0, 3, 1, 4).reshape(2, N, N)
    spectrum = jnp.fft.ifft2(grid[0] + 1j * grid[1])
    return (jnp.real(spectrum) * N).T.astype(jnp.float32)
```

```python
import numpy as np
import jax
import jax.numpy as jnp
from jax import lax
from jax.experimental import pallas as pl
from jax.experimental.pallas import tpu as pltpu
from jax.sharding import PartitionSpec as P

N = 8192
P_SIZE = 128
CAP = 4
SIDE = N // P_SIZE
BAND = 4
SPREAD = 0.75
F32 = jnp.float32
BF16 = jnp.bfloat16
GAUSS = -1.0 / (2.0 * SPREAD * SPREAD * np.log(2.0))
VMEM_LIMIT = 56 * 1024 * 1024


def angle_tables(rows, cols, length):
    angles = 2.0 * np.pi * ((rows[:, None] * cols[None, :]) % length) / length
    return np.cos(angles), np.sin(angles)


def complex_matrix(cosine, sine):
    return np.block([[cosine, -sine], [sine, cosine]])


def split_table(table):
    high = table.astype(np.float32).astype(BF16)
    low = (table - high.astype(np.float64)).astype(np.float32).astype(BF16)
    return high, low


def row_tables():
    dft_hi, dft_lo = split_table(
        complex_matrix(*angle_tables(np.arange(128), np.arange(128), 128))
    )
    twist_cos, twist_sin = angle_tables(np.arange(64), np.arange(128), N)
    return dft_hi, dft_lo, twist_cos.astype(np.float32), twist_sin.astype(np.float32)


def column_tables():
    order = (np.arange(256) % 16) * 16 + np.arange(256) // 16
    first = complex_matrix(*angle_tables(np.arange(256), order, 256)) / N
    first_hi, first_lo = split_table(first)
    lane_r = np.arange(128) % 32
    twist_cos, twist_sin = angle_tables(np.arange(256), lane_r, N)
    cos_r, sin_r = angle_tables(np.arange(32), np.arange(32), 32)
    last = np.concatenate(
        [np.kron(np.eye(4), cos_r), -np.kron(np.eye(4), sin_r)], axis=1
    )
    last_hi, last_lo = split_table(last)
    return (
        first_hi,
        first_lo,
        twist_cos.astype(np.float32),
        twist_sin.astype(np.float32),
        last_hi,
        last_lo,
    )


def split_value(value):
    high = value.astype(BF16)
    low = (value - high.astype(F32)).astype(BF16)
    return high, low


def nt_dot(left, right):
    return lax.dot_general(
        left, right, (((1,), (1,)), ((), ())), preferred_element_type=F32
    )


def pick_kernel(ids_ref, source_ref, out_ref, sem):
    count = out_ref.shape[0]

    def start(i, carry):
        pltpu.make_async_copy(source_ref.at[ids_ref[i]], out_ref.at[i], sem).start()
        return carry

    lax.fori_loop(0, count, start, 0)
    pltpu.make_async_copy(source_ref.at[pl.ds(0, count)], out_ref, sem).wait()


def pick_blocks(ids, source):
    count = ids.shape[0]
    return pl.pallas_call(
        pick_kernel,
        out_shape=jax.ShapeDtypeStruct((count,) + source.shape[1:], source.dtype),
        grid_spec=pltpu.PrefetchScalarGridSpec(
            num_scalar_prefetch=1,
            grid=(1,),
            in_specs=[pl.BlockSpec(memory_space=pl.ANY)],
            out_specs=pl.BlockSpec(memory_space=pl.ANY),
            scratch_shapes=[pltpu.SemaphoreType.DMA],
        ),
        name="pick_blocks",
    )(ids, source)


def grid_kernel(order_ref, slot_ref, count_ref, vis_ref, out_ref, acc_ref):
    acc_ref[...] = jnp.zeros_like(acc_ref)
    cells = lax.broadcasted_iota(jnp.int32, (P_SIZE, 128), 0).astype(F32)
    count = count_ref[0]

    def one_block(at, live):
        entry = order_ref[at]
        slot = slot_ref[at]
        values = vis_ref[entry].astype(F32)
        keep = jnp.where(live, 1.0, 0.0).astype(F32)
        real = values[0:8] * keep
        imag = values[8:16] * keep
        place_u = values[16:24]
        place_v = values[24:32]
        total = jnp.zeros((2 * P_SIZE, P_SIZE), F32)
        for pair in range(4):
            left = []
            right = []
            for k in (2 * pair, 2 * pair + 1):
                gap_u = cells - place_u[k : k + 1]
                row = jnp.exp2(gap_u * gap_u * GAUSS)
                left.append(
                    jnp.concatenate(
                        [
                            (real[k : k + 1] * row).astype(BF16),
                            (imag[k : k + 1] * row).astype(BF16),
                        ],
                        axis=0,
                    )
                )
                gap_v = cells - place_v[k : k + 1]
                right.append(jnp.exp2(gap_v * gap_v * GAUSS).astype(BF16))
            total += nt_dot(
                jnp.concatenate(left, axis=1), jnp.concatenate(right, axis=1)
            )
        acc_ref[slot] += total.astype(BF16).astype(F32)

    def step(i, carry):
        one_block(2 * i, True)
        one_block(2 * i + 1, 2 * i + 1 < count)
        return carry

    lax.fori_loop(0, (count + 1) // 2, step, 0)
    for slot in range(BAND * BAND):
        sub_row, sub_col = divmod(slot, BAND)
        for part in range(2):
            for piece in range(4):
                start = part * P_SIZE + piece * 32
                out_ref[
                    4 * sub_row + piece, part, :, sub_col * P_SIZE : (sub_col + 1) * P_SIZE
                ] = acc_ref[slot, start : start + 32, :].astype(BF16)


def grid_blocks(order, slots, count, vis):
    whole = lambda *_: (0, 0, 0)
    return pl.pallas_call(
        grid_kernel,
        out_shape=jax.ShapeDtypeStruct((16, 2, 32, 512), BF16),
        grid_spec=pltpu.PrefetchScalarGridSpec(
            num_scalar_prefetch=3,
            grid=(1,),
            in_specs=[pl.BlockSpec(vis.shape, whole)],
            out_specs=pl.BlockSpec((16, 2, 32, 512), lambda *_: (0, 0, 0, 0)),
            scratch_shapes=[pltpu.VMEM((BAND * BAND, 2 * P_SIZE, P_SIZE), F32)],
        ),
        compiler_params=pltpu.CompilerParams(vmem_limit_bytes=VMEM_LIMIT),
        name="grid_blocks",
    )(order, slots, count, vis)


def add(x, y):
    return x[0] + y[0], x[1] + y[1]


def sub(x, y):
    return x[0] - y[0], x[1] - y[1]


def turn(x):
    return -x[1], x[0]


def scale(x, numer, denom):
    numer %= denom
    if numer == 0:
        return x
    if 4 * numer == denom:
        return turn(x)
    if 2 * numer == denom:
        return -x[0], -x[1]
    if 4 * numer == 3 * denom:
        return x[1], -x[0]
    cosine = float(np.cos(2 * np.pi * numer / denom))
    sine = float(np.sin(2 * np.pi * numer / denom))
    return x[0] * cosine - x[1] * sine, x[0] * sine + x[1] * cosine


def dft4(x0, x1, x2, x3):
    even_sum, even_diff = add(x0, x2), sub(x0, x2)
    odd_sum, odd_diff = add(x1, x3), turn(sub(x1, x3))
    return (
        add(even_sum, odd_sum),
        add(even_diff, odd_diff),
        sub(even_sum, odd_sum),
        sub(even_diff, odd_diff),
    )


def dft16(items):
    firsts = [dft4(*[items[4 * j1 + j2] for j1 in range(4)]) for j2 in range(4)]
    result = [None] * 16
    for b1 in range(4):
        lasts = dft4(*[scale(firsts[j2][b1], j2 * b1, 16) for j2 in range(4)])
        for b2 in range(4):
            result[b1 + 4 * b2] = lasts[b2]
    return result


def row_kernel(
    x_ref, dft_hi_ref, dft_lo_ref, cos_ref, sin_ref, out_ref, mid_ref, hi_ref, lo_ref, put_ref
):
    for half in range(2):
        rows = pl.ds(16 * half, 16)
        for kappa in range(4):
            lanes = pl.ds(128 * kappa, 128)
            items = [
                (x_ref[j, 0, rows, lanes].astype(F32), x_ref[j, 1, rows, lanes].astype(F32))
                for j in range(16)
            ]
            for a1, item in enumerate(dft16(items)):
                item = scale(item, kappa * a1, 64)
                mid_ref[kappa, a1, 0, rows, :] = item[0]
                mid_ref[kappa, a1, 1, rows, :] = item[1]
    for a1 in range(16):
        items = [(mid_ref[kappa, a1, 0], mid_ref[kappa, a1, 1]) for kappa in range(4)]
        for a2, item in enumerate(dft4(*items)):
            a = a1 + 16 * a2
            cosine = cos_ref[a : a + 1, :]
            sine = sin_ref[a : a + 1, :]
            real = item[0] * cosine - item[1] * sine
            imag = item[0] * sine + item[1] * cosine
            both = jnp.concatenate([real, imag], axis=1)
            high, low = split_value(both)
            hi_ref[a * 32 : (a + 1) * 32, :] = high
            lo_ref[a * 32 : (a + 1) * 32, :] = low
    dft_hi = dft_hi_ref[...]
    dft_lo = dft_lo_ref[...]
    for n in range(8):
        high = hi_ref[n * 256 : (n + 1) * 256, :]
        low = lo_ref[n * 256 : (n + 1) * 256, :]
        made = nt_dot(dft_hi, high) + nt_dot(dft_lo, high) + nt_dot(dft_hi, low)
        for part in range(2):
            for piece in range(2):
                half, i = divmod(2 * n + piece, 8)
                put_ref[pl.ds(half * 16 + part * 8 + i, 128, stride=32), :] = made[
                    part * 128 : (part + 1) * 128, piece * 128 : (piece + 1) * 128
                ]
    out_ref[...] = put_ref[...].reshape(256, 16, 128).astype(BF16)


def row_transform(x):
    tables = [jnp.asarray(t) for t in row_tables()]
    return pl.pallas_call(
        row_kernel,
        out_shape=jax.ShapeDtypeStruct((256, 16, 128), BF16),
        scratch_shapes=[
            pltpu.VMEM((4, 16, 2, 32, 128), F32),
            pltpu.VMEM((2048, 256), BF16),
            pltpu.VMEM((2048, 256), BF16),
            pltpu.VMEM((4096, 128), F32),
        ],
        compiler_params=pltpu.CompilerParams(vmem_limit_bytes=VMEM_LIMIT),
        name="row_transform",
    )(x, *tables)


def column_kernel(
    x_ref, first_hi_ref, first_lo_ref, cos_ref, sin_ref, last_hi_ref, last_lo_ref, out_ref, get_ref, put_ref
):
    get_ref[...] = x_ref[...].astype(F32).reshape(4096, 128)
    first_hi = first_hi_ref[...]
    first_lo = first_lo_ref[...]
    last_hi = last_hi_ref[...]
    last_lo = last_lo_ref[...]
    cosine = cos_ref[...]
    sine = sin_ref[...]
    for g in range(8):
        x = jnp.concatenate(
            [
                get_ref[pl.ds(g, 256, stride=16), :].astype(BF16),
                get_ref[pl.ds(8 + g, 256, stride=16), :].astype(BF16),
            ],
            axis=0,
        )
        mid = jnp.dot(first_hi, x, preferred_element_type=F32) + jnp.dot(
            first_lo, x, preferred_element_type=F32
        )
        real, imag = mid[:256], mid[256:]
        both = jnp.concatenate(
            [real * cosine - imag * sine, real * sine + imag * cosine], axis=1
        )
        high, low = split_value(both)
        made = nt_dot(last_hi, high) + nt_dot(last_lo, high) + nt_dot(last_hi, low)
        for side in range(2):
            start = side * 1024 + g * 128
            put_ref[start : start + 128, :] = made[:, side * 128 : (side + 1) * 128]
    for gamma in range(32):
        for side in range(2):
            start = gamma * 256 + side * 128
            out_ref[:, start : start + 128] = put_ref[
                pl.ds(side * 1024 + gamma, 32, stride=32), :
            ]


def column_transform(x):
    tables = [jnp.asarray(t) for t in column_tables()]
    return pl.pallas_call(
        column_kernel,
        out_shape=jax.ShapeDtypeStruct((32, N), F32),
        scratch_shapes=[pltpu.VMEM((4096, 128), F32), pltpu.VMEM((2048, 128), F32)],
        compiler_params=pltpu.CompilerParams(vmem_limit_bytes=VMEM_LIMIT),
        name="column_transform",
    )(x, *tables)


def block_of(index):
    row = index // SIDE
    col = index % SIDE
    return row // BAND, col // BAND, row % BAND * BAND + col % BAND


def send_ids(own_row, facet_id):
    band, column, slot = block_of(own_row)
    key = band * 16 + column
    number = jnp.arange(own_row.shape[0], dtype=jnp.int32)
    same = (key[None, :] == key[:, None]) & (number[None, :] < number[:, None])
    rank = jnp.sum(same.astype(jnp.int32), axis=1)
    want_band = jnp.repeat(jnp.arange(16, dtype=jnp.int32), CAP)[:, None]
    want_rank = jnp.tile(jnp.arange(CAP, dtype=jnp.int32), 16)[:, None]
    hit = (key[None, :] == want_band * 16 + facet_id) & (rank[None, :] == want_rank)
    return jnp.sum(jnp.where(hit, number[None, :], 0), axis=1)


def receive_table(sub_index, my_band, my_column):
    band, column, slot = block_of(sub_index)
    inside = (band == my_band) & (column == my_column)
    count = sub_index.shape[1]
    before = (
        jnp.arange(count)[:, None] < jnp.arange(count)[None, :]
    ).astype(BF16)
    rank = jnp.dot(inside.astype(BF16), before, preferred_element_type=F32)
    hit = inside[:, None, :] & (rank[:, None, :] == jnp.arange(CAP, dtype=F32)[None, :, None])
    filled = jnp.any(hit, axis=2).reshape(-1)
    slots = jnp.sum(jnp.where(hit, slot[:, None, :], 0), axis=2).reshape(-1)
    entries = filled.shape[0]
    number = jnp.arange(entries, dtype=jnp.int32)
    place = jnp.sum(
        ((number[None, :] < number[:, None]) & filled[None, :]).astype(jnp.int32), axis=1
    )
    chosen = filled[None, :] & (place[None, :] == number[:, None])
    order = jnp.sum(jnp.where(chosen, number[None, :], 0), axis=1)
    sorted_slots = jnp.sum(jnp.where(chosen, slots[None, :], 0), axis=1)
    total = jnp.sum(filled.astype(jnp.int32)).reshape(1)
    return order, sorted_slots, total


def shards(visibilities, coordinates, phases, sub_index):
    facet_id = lax.axis_index("facet")
    span_id = lax.axis_index("span")
    blocks = visibilities.shape[1]
    with jax.named_scope("rotate"):
        vis = visibilities[0].reshape(blocks, 2, 8, 128).astype(F32)
        place = coordinates[0].reshape(blocks, 16, 128)
        angle = phases[0].reshape(blocks, 8, 128)
        cosine = jnp.cos(angle)
        sine = jnp.sin(angle)
        real = vis[:, 0] * cosine - vis[:, 1] * sine
        imag = vis[:, 0] * sine + vis[:, 1] * cosine
        records = jnp.concatenate([real.astype(BF16), imag.astype(BF16), place], axis=1)
    with jax.named_scope("gather_span"):
        everything = lax.all_gather(records, "facet", axis=0, tiled=True)
    with jax.named_scope("choose"):
        own_row = lax.dynamic_index_in_dim(sub_index, span_id, 0, keepdims=False)
        chosen = pick_blocks(send_ids(own_row, facet_id), everything)
        order, slots, count = receive_table(sub_index, span_id, facet_id)
    with jax.named_scope("to_owner"):
        arrived = lax.all_to_all(
            chosen.reshape(16, CAP, 32, 128), "span", split_axis=0, concat_axis=0, tiled=True
        )
    with jax.named_scope("gridding"):
        block = grid_blocks(order, slots, count, arrived.reshape(16 * CAP, 32, 128))
    with jax.named_scope("to_rows"):
        rows = lax.all_to_all(block, "facet", split_axis=0, concat_axis=0, tiled=True)
    with jax.named_scope("rows_dft"):
        half_done = row_transform(rows)
    with jax.named_scope("to_columns"):
        columns = lax.all_to_all(
            half_done, ("facet", "span"), split_axis=0, concat_axis=0, tiled=True
        )
    with jax.named_scope("columns_dft"):
        return column_transform(columns)


def solution(mesh):
    return jax.shard_map(
        shards,
        mesh=mesh,
        in_specs=(
            P("span", "facet", None, None),
            P("span", "facet", None, None),
            P("span", "facet", None),
            P(),
        ),
        out_specs=P(("facet", "span"), None),
        check_vma=False,
    )
```

```python
import numpy as np
import jax
import jax.numpy as jnp
from jax import lax
from jax.experimental import pallas as pl
from jax.experimental.pallas import tpu as pltpu
from jax.sharding import PartitionSpec as P

N = 8192
P_SIZE = 128
CAP = 4
STEP = 8
GAP = 264
SIDE = N // P_SIZE
BAND = 4
SPREAD = 0.75
F32 = jnp.float32
BF16 = jnp.bfloat16
GAUSS = -1.0 / (2.0 * SPREAD * SPREAD * np.log(2.0))
VMEM_LIMIT = 56 * 1024 * 1024


def angle_tables(rows, cols, length):
    angles = 2.0 * np.pi * ((rows[:, None] * cols[None, :]) % length) / length
    return np.cos(angles), np.sin(angles)


def complex_matrix(cosine, sine):
    return np.block([[cosine, -sine], [sine, cosine]])


def split_table(table):
    high = table.astype(np.float32).astype(BF16)
    low = (table - high.astype(np.float64)).astype(np.float32).astype(BF16)
    return high, low


def row_tables():
    dft_hi, dft_lo = split_table(
        complex_matrix(*angle_tables(np.arange(128), np.arange(128), 128))
    )
    twist_cos, twist_sin = angle_tables(np.arange(64), np.arange(128), N)
    return dft_hi, dft_lo, twist_cos.astype(np.float32), twist_sin.astype(np.float32)


def column_tables():
    lane_r = np.arange(128) % 32
    twist_cos, twist_sin = angle_tables(np.arange(256), lane_r, N)
    cos_r, sin_r = angle_tables(np.arange(32), np.arange(32), 32)
    last = np.concatenate(
        [np.kron(np.eye(4), cos_r), -np.kron(np.eye(4), sin_r)], axis=1
    )
    last_hi, last_lo = split_table(last)
    return (
        (twist_cos / N).astype(np.float32),
        (twist_sin / N).astype(np.float32),
        last_hi,
        last_lo,
    )


def split_value(value):
    high = value.astype(BF16)
    low = (value - high.astype(F32)).astype(BF16)
    return high, low


def nt_dot(left, right):
    return lax.dot_general(
        left, right, (((1,), (1,)), ((), ())), preferred_element_type=F32
    )


def rotate_kernel(vis0_ref, vis1_ref, u_ref, v_ref, phase_ref, out_ref):
    for k in range(8):
        lanes = pl.ds(128 * k, 128)
        phase = phase_ref[:, lanes]
        cosine = jnp.cos(phase)
        sine = jnp.sin(phase)
        real = vis0_ref[:, lanes].astype(F32)
        imag = vis1_ref[:, lanes].astype(F32)
        out_ref[2 * k, :, :128] = (real * cosine - imag * sine).astype(BF16)
        out_ref[2 * k, :, 128:] = (real * sine + imag * cosine).astype(BF16)
        out_ref[2 * k + 1, :, :128] = u_ref[:, lanes]
        out_ref[2 * k + 1, :, 128:] = v_ref[:, lanes]


def rotate_blocks(visibilities, coordinates, phases):
    blocks = phases.shape[0]
    return pl.pallas_call(
        rotate_kernel,
        out_shape=jax.ShapeDtypeStruct((16, blocks, 256), BF16),
        name="rotate_blocks",
    )(
        visibilities[:, 0],
        visibilities[:, 1],
        coordinates[:, 0],
        coordinates[:, 1],
        phases,
    )


def pick_kernel(code_ref, rows_ref, out_ref, put_ref):
    wanted = lax.broadcasted_iota(jnp.int32, (256, 512), 0)
    for piece in range(4):
        hit = jnp.where(code_ref[...] == wanted + 256 * piece, 1.0, 0.0).astype(BF16)
        for half in range(2):
            made = jnp.dot(
                hit, rows_ref[:, half * 128 : (half + 1) * 128], preferred_element_type=F32
            )
            put_ref[pl.ds(512 * piece + half, 256, stride=2), :] = made
    out_ref[...] = put_ref[...].reshape(256, 8, 128).astype(BF16)


def pick_blocks(code, rows):
    return pl.pallas_call(
        pick_kernel,
        out_shape=jax.ShapeDtypeStruct((256, 8, 128), BF16),
        scratch_shapes=[pltpu.VMEM((2048, 128), F32)],
        compiler_params=pltpu.CompilerParams(vmem_limit_bytes=VMEM_LIMIT),
        name="pick_blocks",
    )(code, rows)


def grid_kernel(order_ref, slot_ref, count_ref, vis_ref, out_ref, wide_ref, acc_ref):
    acc_ref[...] = jnp.zeros_like(acc_ref)
    wide_ref[...] = vis_ref[...].astype(F32).reshape(2048, 128)
    cells = lax.broadcasted_iota(jnp.int32, (P_SIZE, 128), 0).astype(F32)
    count = count_ref[0]

    def one_block(at, live):
        entry = order_ref[at]
        slot = slot_ref[at]
        keep = jnp.where(live, 1.0, 0.0).astype(F32)
        first = wide_ref[pl.ds(2 * entry, 16, stride=128), :]
        second = wide_ref[pl.ds(2 * entry + 1, 16, stride=128), :]
        total = None
        for pair in range(4):
            left = []
            right = []
            for k in (2 * pair, 2 * pair + 1):
                real = (first[2 * k : 2 * k + 1] * keep).astype(BF16)
                imag = (second[2 * k : 2 * k + 1] * keep).astype(BF16)
                gap_u = cells - first[2 * k + 1 : 2 * k + 2]
                row = jnp.exp2(gap_u * gap_u * GAUSS).astype(BF16)
                left.append(jnp.concatenate([row * real, row * imag], axis=0))
                gap_v = cells - second[2 * k + 1 : 2 * k + 2]
                right.append(jnp.exp2(gap_v * gap_v * GAUSS).astype(BF16))
            made = nt_dot(
                jnp.concatenate(left, axis=1), jnp.concatenate(right, axis=1)
            )
            total = made if total is None else total + made
        acc_ref[slot] += total.astype(BF16).astype(F32)

    def step(i, carry):
        for t in range(STEP):
            one_block(STEP * i + t, STEP * i + t < count)
        return carry

    lax.fori_loop(0, (count + STEP - 1) // STEP, step, 0)
    for slot in range(BAND * BAND):
        sub_row, sub_col = divmod(slot, BAND)
        for part in range(2):
            for piece in range(4):
                start = part * P_SIZE + piece * 32
                out_ref[
                    4 * sub_row + piece, part, :, sub_col * P_SIZE : (sub_col + 1) * P_SIZE
                ] = acc_ref[slot, start : start + 32, :].astype(BF16)


def grid_blocks(order, slots, count, vis):
    whole = lambda *_: (0, 0, 0)
    return pl.pallas_call(
        grid_kernel,
        out_shape=jax.ShapeDtypeStruct((16, 2, 32, 512), BF16),
        grid_spec=pltpu.PrefetchScalarGridSpec(
            num_scalar_prefetch=3,
            grid=(1,),
            in_specs=[pl.BlockSpec(vis.shape, whole)],
            out_specs=pl.BlockSpec((16, 2, 32, 512), lambda *_: (0, 0, 0, 0)),
            scratch_shapes=[
                pltpu.VMEM((2048, 128), F32),
                pltpu.VMEM((BAND * BAND, 2 * P_SIZE, P_SIZE), F32),
            ],
        ),
        compiler_params=pltpu.CompilerParams(vmem_limit_bytes=VMEM_LIMIT),
        name="grid_blocks",
    )(order, slots, count, vis)


def add(x, y):
    return x[0] + y[0], x[1] + y[1]


def sub(x, y):
    return x[0] - y[0], x[1] - y[1]


def turn(x):
    return -x[1], x[0]


def scale(x, numer, denom):
    numer %= denom
    if numer == 0:
        return x
    if 4 * numer == denom:
        return turn(x)
    if 2 * numer == denom:
        return -x[0], -x[1]
    if 4 * numer == 3 * denom:
        return x[1], -x[0]
    cosine = float(np.cos(2 * np.pi * numer / denom))
    sine = float(np.sin(2 * np.pi * numer / denom))
    return x[0] * cosine - x[1] * sine, x[0] * sine + x[1] * cosine


def dft4(x0, x1, x2, x3):
    even_sum, even_diff = add(x0, x2), sub(x0, x2)
    odd_sum, odd_diff = add(x1, x3), turn(sub(x1, x3))
    return (
        add(even_sum, odd_sum),
        add(even_diff, odd_diff),
        sub(even_sum, odd_sum),
        sub(even_diff, odd_diff),
    )


def dft16(items):
    firsts = [dft4(*[items[4 * j1 + j2] for j1 in range(4)]) for j2 in range(4)]
    result = [None] * 16
    for b1 in range(4):
        lasts = dft4(*[scale(firsts[j2][b1], j2 * b1, 16) for j2 in range(4)])
        for b2 in range(4):
            result[b1 + 4 * b2] = lasts[b2]
    return result


def row_kernel(
    x_ref, dft_hi_ref, dft_lo_ref, cos_ref, sin_ref, out_ref, mid_ref, hi_ref, lo_ref, put_ref
):
    for half in range(2):
        rows = pl.ds(16 * half, 16)
        for kappa in range(4):
            lanes = pl.ds(128 * kappa, 128)
            items = [
                (x_ref[j, 0, rows, lanes].astype(F32), x_ref[j, 1, rows, lanes].astype(F32))
                for j in range(16)
            ]
            for a1, item in enumerate(dft16(items)):
                item = scale(item, kappa * a1, 64)
                mid_ref[kappa, a1, 0, rows, :] = item[0]
                mid_ref[kappa, a1, 1, rows, :] = item[1]
    for a1 in range(16):
        items = [(mid_ref[kappa, a1, 0], mid_ref[kappa, a1, 1]) for kappa in range(4)]
        for a2, item in enumerate(dft4(*items)):
            a = a1 + 16 * a2
            cosine = cos_ref[a : a + 1, :]
            sine = sin_ref[a : a + 1, :]
            real = item[0] * cosine - item[1] * sine
            imag = item[0] * sine + item[1] * cosine
            both = jnp.concatenate([real, imag], axis=1)
            high, low = split_value(both)
            hi_ref[a * 32 : (a + 1) * 32, :] = high
            lo_ref[a * 32 : (a + 1) * 32, :] = low
    dft_hi = dft_hi_ref[...]
    dft_lo = dft_lo_ref[...]
    for n in range(8):
        high = hi_ref[n * 256 : (n + 1) * 256, :]
        low = lo_ref[n * 256 : (n + 1) * 256, :]
        made = nt_dot(dft_hi, high) + nt_dot(dft_lo, high) + nt_dot(dft_hi, low)
        for part in range(2):
            for piece in range(2):
                half, i = divmod(2 * n + piece, 8)
                put_ref[pl.ds(half * 16 + part * 8 + i, 128, stride=32), :] = made[
                    part * 128 : (part + 1) * 128, piece * 128 : (piece + 1) * 128
                ]
    out_ref[...] = put_ref[...].reshape(256, 16, 128).astype(BF16)


def row_transform(x):
    tables = [jnp.asarray(t) for t in row_tables()]
    return pl.pallas_call(
        row_kernel,
        out_shape=jax.ShapeDtypeStruct((256, 16, 128), BF16),
        scratch_shapes=[
            pltpu.VMEM((4, 16, 2, 32, 128), F32),
            pltpu.VMEM((2048, 256), BF16),
            pltpu.VMEM((2048, 256), BF16),
            pltpu.VMEM((4096, 128), F32),
        ],
        compiler_params=pltpu.CompilerParams(vmem_limit_bytes=VMEM_LIMIT),
        name="row_transform",
    )(x, *tables)


def column_kernel(
    x_ref, cos_ref, sin_ref, last_hi_ref, last_lo_ref, out_ref, mid_ref, real_ref, imag_ref, put_ref
):
    for chunk in range(16):
        items = []
        for band in range(16):
            value = x_ref[chunk * 16 + band].astype(F32)
            items.append((value[:8], value[8:]))
        for first, item in enumerate(dft16(items)):
            item = scale(item, first * chunk, 256)
            mid_ref[first, chunk, 0] = item[0]
            mid_ref[first, chunk, 1] = item[1]
    for first in range(16):
        items = [(mid_ref[first, chunk, 0], mid_ref[first, chunk, 1]) for chunk in range(16)]
        for second, item in enumerate(dft16(items)):
            at = first + 16 * second
            cosine = cos_ref[at : at + 1, :]
            sine = sin_ref[at : at + 1, :]
            rows = pl.ds(at, 8, stride=GAP)
            real_ref[rows, :] = item[0] * cosine - item[1] * sine
            imag_ref[rows, :] = item[0] * sine + item[1] * cosine
    last_hi = last_hi_ref[...]
    last_lo = last_lo_ref[...]
    for g in range(8):
        both = jnp.concatenate(
            [real_ref[g * GAP : g * GAP + 256, :], imag_ref[g * GAP : g * GAP + 256, :]], axis=1
        )
        high, low = split_value(both)
        made = nt_dot(last_hi, high) + nt_dot(last_lo, high) + nt_dot(last_hi, low)
        for side in range(2):
            start = side * 1024 + g * 128
            put_ref[start : start + 128, :] = made[:, side * 128 : (side + 1) * 128]
    for gamma in range(32):
        for side in range(2):
            start = gamma * 256 + side * 128
            out_ref[:, start : start + 128] = put_ref[
                pl.ds(side * 1024 + gamma, 32, stride=32), :
            ]


def column_transform(x):
    tables = [jnp.asarray(t) for t in column_tables()]
    return pl.pallas_call(
        column_kernel,
        out_shape=jax.ShapeDtypeStruct((32, N), F32),
        scratch_shapes=[
            pltpu.VMEM((16, 16, 2, 8, 128), F32),
            pltpu.VMEM((8 * GAP, 128), F32),
            pltpu.VMEM((8 * GAP, 128), F32),
            pltpu.VMEM((2048, 128), F32),
        ],
        compiler_params=pltpu.CompilerParams(vmem_limit_bytes=VMEM_LIMIT),
        name="column_transform",
    )(x, *tables)


def block_of(index):
    row = index // SIDE
    col = index % SIDE
    return row // BAND, col // BAND, row % BAND * BAND + col % BAND


def send_code(own_row):
    band, column, slot = block_of(own_row)
    key = column * 16 + band
    number = jnp.arange(own_row.shape[0], dtype=jnp.int32)
    same = (key[None, :] == key[:, None]) & (number[:, None] < number[None, :])
    rank = jnp.sum(same.astype(jnp.int32), axis=0)
    return (key * CAP + rank)[None, :]


def receive_table(sub_index, my_band, my_column):
    band, column, slot = block_of(sub_index)
    inside = (band == my_band) & (column == my_column)
    count = sub_index.shape[1]
    before = (
        jnp.arange(count)[:, None] < jnp.arange(count)[None, :]
    ).astype(BF16)
    rank = jnp.dot(inside.astype(BF16), before, preferred_element_type=F32)
    hit = inside[:, None, :] & (rank[:, None, :] == jnp.arange(CAP, dtype=F32)[None, :, None])
    filled = jnp.any(hit, axis=2).reshape(-1)
    slots = jnp.sum(jnp.where(hit, slot[:, None, :], 0), axis=2).reshape(-1)
    entries = filled.shape[0]
    number = jnp.arange(entries, dtype=jnp.int32)
    place = jnp.sum(
        ((number[None, :] < number[:, None]) & filled[None, :]).astype(jnp.int32), axis=1
    )
    chosen = filled[None, :] & (place[None, :] == number[:, None])
    order = jnp.sum(jnp.where(chosen, number[None, :], 0), axis=1)
    sorted_slots = jnp.sum(jnp.where(chosen, slots[None, :], 0), axis=1)
    total = jnp.sum(filled.astype(jnp.int32)).reshape(1)
    return order, sorted_slots, total


def shards(visibilities, coordinates, phases, sub_index):
    facet_id = lax.axis_index("facet")
    span_id = lax.axis_index("span")
    with jax.named_scope("rotate"):
        parts = rotate_blocks(visibilities[0], coordinates[0], phases[0])
    with jax.named_scope("spread_span"):
        spread = lax.all_to_all(parts, "facet", split_axis=0, concat_axis=0, tiled=True)
    with jax.named_scope("choose"):
        own_row = lax.dynamic_index_in_dim(sub_index, span_id, 0, keepdims=False)
        chosen = pick_blocks(send_code(own_row), spread.reshape(-1, 256))
        order, slots, count = receive_table(sub_index, span_id, facet_id)
    with jax.named_scope("to_owner"):
        arrived = lax.all_to_all(
            chosen, ("facet", "span"), split_axis=0, concat_axis=0, tiled=True
        )
    with jax.named_scope("gridding"):
        block = grid_blocks(order, slots, count, arrived)
    with jax.named_scope("to_rows"):
        rows = lax.all_to_all(block, "facet", split_axis=0, concat_axis=0, tiled=True)
    with jax.named_scope("rows_dft"):
        half_done = row_transform(rows)
    with jax.named_scope("to_columns"):
        columns = lax.all_to_all(
            half_done, ("facet", "span"), split_axis=0, concat_axis=0, tiled=True
        )
    with jax.named_scope("columns_dft"):
        return column_transform(columns)


def solution(mesh):
    return jax.shard_map(
        shards,
        mesh=mesh,
        in_specs=(
            P("span", "facet", None, None),
            P("span", "facet", None, None),
            P("span", "facet", None),
            P(),
        ),
        out_specs=P(("facet", "span"), None),
        check_vma=False,
    )
```

```python
import numpy as np
import jax
import jax.numpy as jnp
from jax import lax
from jax.experimental import pallas as pl
from jax.experimental.pallas import tpu as pltpu
from jax.sharding import PartitionSpec as P

N = 8192
P_SIZE = 128
CAP = 4
STEP = 8
GAP = 264
SIDE = N // P_SIZE
BAND = 4
SPREAD = 0.75
F32 = jnp.float32
BF16 = jnp.bfloat16
GAUSS = -1.0 / (2.0 * SPREAD * SPREAD * np.log(2.0))
VMEM_LIMIT = 24 * 1024 * 1024
LOCAL = pl.BlockSpec(memory_space=pltpu.VMEM)


def angle_tables(rows, cols, length):
    angles = 2.0 * np.pi * ((rows[:, None] * cols[None, :]) % length) / length
    return np.cos(angles), np.sin(angles)


def complex_matrix(cosine, sine):
    return np.block([[cosine, -sine], [sine, cosine]])


def split_table(table):
    high = table.astype(np.float32).astype(BF16)
    low = (table - high.astype(np.float64)).astype(np.float32).astype(BF16)
    return high, low


def row_tables():
    dft_hi, dft_lo = split_table(
        complex_matrix(*angle_tables(np.arange(128), np.arange(128), 128))
    )
    twist_cos, twist_sin = angle_tables(np.arange(64), np.arange(128), N)
    return dft_hi, dft_lo, twist_cos.astype(np.float32), twist_sin.astype(np.float32)


def column_tables():
    lane_r = np.arange(128) % 32
    twist_cos, twist_sin = angle_tables(np.arange(256), lane_r, N)
    cos_r, sin_r = angle_tables(np.arange(32), np.arange(32), 32)
    last = np.concatenate(
        [np.kron(np.eye(4), cos_r), -np.kron(np.eye(4), sin_r)], axis=1
    )
    last_hi, last_lo = split_table(last)
    return (
        (twist_cos / N).astype(np.float32),
        (twist_sin / N).astype(np.float32),
        last_hi,
        last_lo,
    )


def split_value(value):
    high = value.astype(BF16)
    low = (value - high.astype(F32)).astype(BF16)
    return high, low


def nt_dot(left, right):
    return lax.dot_general(
        left, right, (((1,), (1,)), ((), ())), preferred_element_type=F32
    )


def rotate_kernel(vis0_ref, vis1_ref, u_ref, v_ref, phase_ref, out_ref):
    for k in range(8):
        lanes = pl.ds(128 * k, 128)
        phase = phase_ref[:, lanes]
        cosine = jnp.cos(phase)
        sine = jnp.sin(phase)
        real = vis0_ref[:, lanes].astype(F32)
        imag = vis1_ref[:, lanes].astype(F32)
        out_ref[2 * k, :, :128] = (real * cosine - imag * sine).astype(BF16)
        out_ref[2 * k, :, 128:] = (real * sine + imag * cosine).astype(BF16)
        out_ref[2 * k + 1, :, :128] = u_ref[:, lanes]
        out_ref[2 * k + 1, :, 128:] = v_ref[:, lanes]


def rotate_blocks(visibilities, coordinates, phases):
    blocks = phases.shape[0]
    return pl.pallas_call(
        rotate_kernel,
        out_shape=jax.ShapeDtypeStruct((16, blocks, 256), BF16),
        in_specs=[LOCAL] * 5,
        out_specs=LOCAL,
        name="rotate_blocks",
    )(
        visibilities[:, 0],
        visibilities[:, 1],
        coordinates[:, 0],
        coordinates[:, 1],
        phases,
    )


def pick_kernel(code_ref, rows_ref, out_ref, put_ref):
    wanted = lax.broadcasted_iota(jnp.int32, (256, 512), 0)
    for piece in range(4):
        hit = jnp.where(code_ref[...] == wanted + 256 * piece, 1.0, 0.0).astype(BF16)
        for half in range(2):
            made = jnp.dot(
                hit, rows_ref[:, half * 128 : (half + 1) * 128], preferred_element_type=F32
            )
            put_ref[pl.ds(512 * piece + half, 256, stride=2), :] = made
    out_ref[...] = put_ref[...].reshape(256, 8, 128).astype(BF16)


def pick_blocks(code, rows):
    return pl.pallas_call(
        pick_kernel,
        out_shape=jax.ShapeDtypeStruct((256, 8, 128), BF16),
        in_specs=[LOCAL] * 2,
        out_specs=LOCAL,
        scratch_shapes=[pltpu.VMEM((2048, 128), F32)],
        compiler_params=pltpu.CompilerParams(vmem_limit_bytes=VMEM_LIMIT),
        name="pick_blocks",
    )(code, rows)


def grid_kernel(order_ref, slot_ref, count_ref, vis_ref, out_ref, wide_ref, acc_ref):
    acc_ref[...] = jnp.zeros_like(acc_ref)
    wide_ref[...] = vis_ref[...].astype(F32).reshape(2048, 128)
    cells = lax.broadcasted_iota(jnp.int32, (P_SIZE, 128), 0).astype(F32)
    count = count_ref[0]

    def one_block(at, live):
        entry = order_ref[at]
        slot = slot_ref[at]
        keep = jnp.where(live, 1.0, 0.0).astype(F32)
        first = wide_ref[pl.ds(2 * entry, 16, stride=128), :]
        second = wide_ref[pl.ds(2 * entry + 1, 16, stride=128), :]
        total = None
        for pair in range(4):
            left = []
            right = []
            for k in (2 * pair, 2 * pair + 1):
                real = (first[2 * k : 2 * k + 1] * keep).astype(BF16)
                imag = (second[2 * k : 2 * k + 1] * keep).astype(BF16)
                gap_u = cells - first[2 * k + 1 : 2 * k + 2]
                row = jnp.exp2(gap_u * gap_u * GAUSS).astype(BF16)
                left.append(jnp.concatenate([row * real, row * imag], axis=0))
                gap_v = cells - second[2 * k + 1 : 2 * k + 2]
                right.append(jnp.exp2(gap_v * gap_v * GAUSS).astype(BF16))
            made = nt_dot(
                jnp.concatenate(left, axis=1), jnp.concatenate(right, axis=1)
            )
            total = made if total is None else total + made
        acc_ref[slot] += total.astype(BF16).astype(F32)

    def step(i, carry):
        for t in range(STEP):
            one_block(STEP * i + t, STEP * i + t < count)
        return carry

    lax.fori_loop(0, (count + STEP - 1) // STEP, step, 0)
    for slot in range(BAND * BAND):
        sub_row, sub_col = divmod(slot, BAND)
        for part in range(2):
            for piece in range(4):
                start = part * P_SIZE + piece * 32
                out_ref[
                    4 * sub_row + piece, part, :, sub_col * P_SIZE : (sub_col + 1) * P_SIZE
                ] = acc_ref[slot, start : start + 32, :].astype(BF16)


def grid_blocks(order, slots, count, vis):
    return pl.pallas_call(
        grid_kernel,
        out_shape=jax.ShapeDtypeStruct((16, 2, 32, 512), BF16),
        in_specs=[pl.BlockSpec(memory_space=pltpu.SMEM)] * 3 + [LOCAL],
        out_specs=LOCAL,
        scratch_shapes=[
            pltpu.VMEM((2048, 128), F32),
            pltpu.VMEM((BAND * BAND, 2 * P_SIZE, P_SIZE), F32),
        ],
        compiler_params=pltpu.CompilerParams(vmem_limit_bytes=VMEM_LIMIT),
        name="grid_blocks",
    )(order, slots, count, vis)


def add(x, y):
    return x[0] + y[0], x[1] + y[1]


def sub(x, y):
    return x[0] - y[0], x[1] - y[1]


def turn(x):
    return -x[1], x[0]


def scale(x, numer, denom):
    numer %= denom
    if numer == 0:
        return x
    if 4 * numer == denom:
        return turn(x)
    if 2 * numer == denom:
        return -x[0], -x[1]
    if 4 * numer == 3 * denom:
        return x[1], -x[0]
    cosine = float(np.cos(2 * np.pi * numer / denom))
    sine = float(np.sin(2 * np.pi * numer / denom))
    return x[0] * cosine - x[1] * sine, x[0] * sine + x[1] * cosine


def dft4(x0, x1, x2, x3):
    even_sum, even_diff = add(x0, x2), sub(x0, x2)
    odd_sum, odd_diff = add(x1, x3), turn(sub(x1, x3))
    return (
        add(even_sum, odd_sum),
        add(even_diff, odd_diff),
        sub(even_sum, odd_sum),
        sub(even_diff, odd_diff),
    )


def dft16(items):
    firsts = [dft4(*[items[4 * j1 + j2] for j1 in range(4)]) for j2 in range(4)]
    result = [None] * 16
    for b1 in range(4):
        lasts = dft4(*[scale(firsts[j2][b1], j2 * b1, 16) for j2 in range(4)])
        for b2 in range(4):
            result[b1 + 4 * b2] = lasts[b2]
    return result


def row_kernel(
    x_ref, dft_hi_ref, dft_lo_ref, cos_ref, sin_ref, out_ref, mid_ref, hi_ref, lo_ref, put_ref
):
    for half in range(2):
        rows = pl.ds(16 * half, 16)
        for kappa in range(4):
            lanes = pl.ds(128 * kappa, 128)
            items = [
                (x_ref[j, 0, rows, lanes].astype(F32), x_ref[j, 1, rows, lanes].astype(F32))
                for j in range(16)
            ]
            for a1, item in enumerate(dft16(items)):
                item = scale(item, kappa * a1, 64)
                mid_ref[kappa, a1, 0, rows, :] = item[0]
                mid_ref[kappa, a1, 1, rows, :] = item[1]
    for a1 in range(16):
        items = [(mid_ref[kappa, a1, 0], mid_ref[kappa, a1, 1]) for kappa in range(4)]
        for a2, item in enumerate(dft4(*items)):
            a = a1 + 16 * a2
            cosine = cos_ref[a : a + 1, :]
            sine = sin_ref[a : a + 1, :]
            real = item[0] * cosine - item[1] * sine
            imag = item[0] * sine + item[1] * cosine
            both = jnp.concatenate([real, imag], axis=1)
            high, low = split_value(both)
            hi_ref[a * 32 : (a + 1) * 32, :] = high
            lo_ref[a * 32 : (a + 1) * 32, :] = low
    dft_hi = dft_hi_ref[...]
    dft_lo = dft_lo_ref[...]
    for n in range(8):
        high = hi_ref[n * 256 : (n + 1) * 256, :]
        low = lo_ref[n * 256 : (n + 1) * 256, :]
        made = nt_dot(dft_hi, high) + nt_dot(dft_lo, high) + nt_dot(dft_hi, low)
        for part in range(2):
            for piece in range(2):
                half, i = divmod(2 * n + piece, 8)
                put_ref[pl.ds(half * 16 + part * 8 + i, 128, stride=32), :] = made[
                    part * 128 : (part + 1) * 128, piece * 128 : (piece + 1) * 128
                ]
    out_ref[...] = put_ref[...].reshape(256, 16, 128).astype(BF16)


def row_transform(x):
    tables = [jnp.asarray(t) for t in row_tables()]
    return pl.pallas_call(
        row_kernel,
        out_shape=jax.ShapeDtypeStruct((256, 16, 128), BF16),
        in_specs=[LOCAL] * (1 + len(tables)),
        out_specs=LOCAL,
        scratch_shapes=[
            pltpu.VMEM((4, 16, 2, 32, 128), F32),
            pltpu.VMEM((2048, 256), BF16),
            pltpu.VMEM((2048, 256), BF16),
            pltpu.VMEM((4096, 128), F32),
        ],
        compiler_params=pltpu.CompilerParams(vmem_limit_bytes=VMEM_LIMIT),
        name="row_transform",
    )(x, *tables)


def column_kernel(
    x_ref, cos_ref, sin_ref, last_hi_ref, last_lo_ref, out_ref, mid_ref, real_ref, imag_ref, put_ref
):
    for chunk in range(16):
        items = []
        for band in range(16):
            value = x_ref[chunk * 16 + band].astype(F32)
            items.append((value[:8], value[8:]))
        for first, item in enumerate(dft16(items)):
            item = scale(item, first * chunk, 256)
            mid_ref[first, chunk, 0] = item[0]
            mid_ref[first, chunk, 1] = item[1]
    for first in range(16):
        items = [(mid_ref[first, chunk, 0], mid_ref[first, chunk, 1]) for chunk in range(16)]
        for second, item in enumerate(dft16(items)):
            at = first + 16 * second
            cosine = cos_ref[at : at + 1, :]
            sine = sin_ref[at : at + 1, :]
            rows = pl.ds(at, 8, stride=GAP)
            real_ref[rows, :] = item[0] * cosine - item[1] * sine
            imag_ref[rows, :] = item[0] * sine + item[1] * cosine
    last_hi = last_hi_ref[...]
    last_lo = last_lo_ref[...]
    for g in range(8):
        both = jnp.concatenate(
            [real_ref[g * GAP : g * GAP + 256, :], imag_ref[g * GAP : g * GAP + 256, :]], axis=1
        )
        high, low = split_value(both)
        made = nt_dot(last_hi, high) + nt_dot(last_lo, high) + nt_dot(last_hi, low)
        for side in range(2):
            start = side * 1024 + g * 128
            put_ref[start : start + 128, :] = made[:, side * 128 : (side + 1) * 128]
    for gamma in range(32):
        for side in range(2):
            start = gamma * 256 + side * 128
            out_ref[:, start : start + 128] = put_ref[
                pl.ds(side * 1024 + gamma, 32, stride=32), :
            ]


def column_transform(x):
    tables = [jnp.asarray(t) for t in column_tables()]
    return pl.pallas_call(
        column_kernel,
        out_shape=jax.ShapeDtypeStruct((32, N), F32),
        in_specs=[LOCAL] * (1 + len(tables)),
        out_specs=LOCAL,
        scratch_shapes=[
            pltpu.VMEM((16, 16, 2, 8, 128), F32),
            pltpu.VMEM((8 * GAP, 128), F32),
            pltpu.VMEM((8 * GAP, 128), F32),
            pltpu.VMEM((2048, 128), F32),
        ],
        compiler_params=pltpu.CompilerParams(vmem_limit_bytes=VMEM_LIMIT),
        name="column_transform",
    )(x, *tables)


def block_of(index):
    row = index // SIDE
    col = index % SIDE
    return row // BAND, col // BAND, row % BAND * BAND + col % BAND


def send_code(own_row):
    band, column, slot = block_of(own_row)
    key = column * 16 + band
    number = jnp.arange(own_row.shape[0], dtype=jnp.int32)
    same = (key[None, :] == key[:, None]) & (number[:, None] < number[None, :])
    rank = jnp.sum(same.astype(jnp.int32), axis=0)
    return (key * CAP + rank)[None, :]


def receive_table(sub_index, my_band, my_column):
    band, column, slot = block_of(sub_index)
    inside = (band == my_band) & (column == my_column)
    count = sub_index.shape[1]
    before = (
        jnp.arange(count)[:, None] < jnp.arange(count)[None, :]
    ).astype(BF16)
    rank = jnp.dot(inside.astype(BF16), before, preferred_element_type=F32)
    hit = inside[:, None, :] & (rank[:, None, :] == jnp.arange(CAP, dtype=F32)[None, :, None])
    filled = jnp.any(hit, axis=2).reshape(-1)
    slots = jnp.sum(jnp.where(hit, slot[:, None, :], 0), axis=2).reshape(-1)
    entries = filled.shape[0]
    number = jnp.arange(entries, dtype=jnp.int32)
    place = jnp.sum(
        ((number[None, :] < number[:, None]) & filled[None, :]).astype(jnp.int32), axis=1
    )
    chosen = filled[None, :] & (place[None, :] == number[:, None])
    order = jnp.sum(jnp.where(chosen, number[None, :], 0), axis=1)
    sorted_slots = jnp.sum(jnp.where(chosen, slots[None, :], 0), axis=1)
    total = jnp.sum(filled.astype(jnp.int32)).reshape(1)
    return order, sorted_slots, total


def shards(visibilities, coordinates, phases, sub_index):
    facet_id = lax.axis_index("facet")
    span_id = lax.axis_index("span")
    with jax.named_scope("rotate"):
        parts = rotate_blocks(visibilities[0], coordinates[0], phases[0])
    with jax.named_scope("spread_span"):
        spread = lax.all_to_all(parts, "facet", split_axis=0, concat_axis=0, tiled=True)
    with jax.named_scope("choose"):
        own_row = lax.dynamic_index_in_dim(sub_index, span_id, 0, keepdims=False)
        chosen = pick_blocks(send_code(own_row), spread.reshape(-1, 256))
        order, slots, count = receive_table(sub_index, span_id, facet_id)
    with jax.named_scope("to_owner"):
        arrived = lax.all_to_all(
            chosen, ("facet", "span"), split_axis=0, concat_axis=0, tiled=True
        )
    with jax.named_scope("gridding"):
        block = grid_blocks(order, slots, count, arrived)
    with jax.named_scope("to_rows"):
        rows = lax.all_to_all(block, "facet", split_axis=0, concat_axis=0, tiled=True)
    with jax.named_scope("rows_dft"):
        half_done = row_transform(rows)
    with jax.named_scope("to_columns"):
        columns = lax.all_to_all(
            half_done, ("facet", "span"), split_axis=0, concat_axis=0, tiled=True
        )
    with jax.named_scope("columns_dft"):
        return column_transform(columns)


def solution(mesh):
    return jax.shard_map(
        shards,
        mesh=mesh,
        in_specs=(
            P("span", "facet", None, None),
            P("span", "facet", None, None),
            P("span", "facet", None),
            P(),
        ),
        out_specs=P(("facet", "span"), None),
        check_vma=False,
    )
```

```python
import numpy as np
import jax
import jax.numpy as jnp
from jax import lax
from jax.experimental import pallas as pl
from jax.experimental.pallas import tpu as pltpu
from jax.sharding import PartitionSpec as P

N = 8192
P_SIZE = 128
CAP = 4
STEP = 8
GAP = 264
PAD = 40
WIDE = 136
SIDE = N // P_SIZE
BAND = 4
SPREAD = 0.75
F32 = jnp.float32
BF16 = jnp.bfloat16
GAUSS = -1.0 / (2.0 * SPREAD * SPREAD * np.log(2.0))
VMEM_LIMIT = 24 * 1024 * 1024
LOCAL = pl.BlockSpec(memory_space=pltpu.VMEM)


def angle_tables(rows, cols, length):
    angles = 2.0 * np.pi * ((rows[:, None] * cols[None, :]) % length) / length
    return np.cos(angles), np.sin(angles)


def complex_matrix(cosine, sine):
    return np.block([[cosine, -sine], [sine, cosine]])


def split_table(table):
    high = table.astype(np.float32).astype(BF16)
    low = (table - high.astype(np.float64)).astype(np.float32).astype(BF16)
    return high, low


def row_tables():
    dft_hi, dft_lo = split_table(
        complex_matrix(*angle_tables(np.arange(128), np.arange(128), 128))
    )
    twist_cos, twist_sin = angle_tables(np.arange(64), np.arange(128), N)
    return dft_hi, dft_lo, twist_cos.astype(np.float32), twist_sin.astype(np.float32)


def column_tables():
    lane_r = np.arange(128) % 32
    twist_cos, twist_sin = angle_tables(np.arange(256), lane_r, N)
    cos_r, sin_r = angle_tables(np.arange(32), np.arange(32), 32)
    last = np.concatenate(
        [np.kron(np.eye(4), cos_r), -np.kron(np.eye(4), sin_r)], axis=1
    )
    last_hi, last_lo = split_table(last)
    return (
        (twist_cos / N).astype(np.float32),
        (twist_sin / N).astype(np.float32),
        last_hi,
        last_lo,
    )


def split_value(value):
    high = value.astype(BF16)
    low = (value - high.astype(F32)).astype(BF16)
    return high, low


def nt_dot(left, right):
    return lax.dot_general(
        left, right, (((1,), (1,)), ((), ())), preferred_element_type=F32
    )


def cos_sin(angle):
    half = angle * 0.5
    square = half * half
    sine = jnp.full_like(half, 1.0 / 6227020800.0)
    for coefficient in (-39916800.0, 362880.0, -5040.0, 120.0, -6.0, 1.0):
        sine = sine * square + 1.0 / coefficient
    sine = sine * half
    cosine = jnp.full_like(half, 1.0 / 479001600.0)
    for coefficient in (-3628800.0, 40320.0, -720.0, 24.0, -2.0, 1.0):
        cosine = cosine * square + 1.0 / coefficient
    return 1.0 - 2.0 * sine * sine, 2.0 * sine * cosine


def rotate_kernel(vis_ref, place_ref, phase_ref, out_ref):
    for k in range(8):
        lanes = pl.ds(128 * k, 128)
        cosine, sine = cos_sin(phase_ref[:, lanes])
        real = vis_ref[:, 0, lanes].astype(F32)
        imag = vis_ref[:, 1, lanes].astype(F32)
        out_ref[2 * k, :, :128] = (real * cosine - imag * sine).astype(BF16)
        out_ref[2 * k, :, 128:] = (real * sine + imag * cosine).astype(BF16)
        out_ref[2 * k + 1, :, :128] = place_ref[:, 0, lanes]
        out_ref[2 * k + 1, :, 128:] = place_ref[:, 1, lanes]


def rotate_blocks(visibilities, coordinates, phases):
    blocks = phases.shape[0]
    return pl.pallas_call(
        rotate_kernel,
        out_shape=jax.ShapeDtypeStruct((16, blocks, 256), BF16),
        in_specs=[LOCAL] * 3,
        out_specs=LOCAL,
        name="rotate_blocks",
    )(visibilities, coordinates, phases)


def pick_kernel(code_ref, rows_ref, out_ref, put_ref):
    wanted = lax.broadcasted_iota(jnp.int32, (256, 512), 0)
    for piece in range(4):
        hit = jnp.where(code_ref[...] == wanted + 256 * piece, 1.0, 0.0).astype(BF16)
        for half in range(2):
            made = jnp.dot(
                hit, rows_ref[:, half * 128 : (half + 1) * 128], preferred_element_type=F32
            )
            put_ref[pl.ds(512 * piece + half, 256, stride=2), :] = made
    out_ref[...] = put_ref[...].reshape(256, 8, 128).astype(BF16)


def pick_blocks(code, rows):
    return pl.pallas_call(
        pick_kernel,
        out_shape=jax.ShapeDtypeStruct((256, 8, 128), BF16),
        in_specs=[LOCAL] * 2,
        out_specs=LOCAL,
        scratch_shapes=[pltpu.VMEM((2048, 128), F32)],
        compiler_params=pltpu.CompilerParams(vmem_limit_bytes=VMEM_LIMIT),
        name="pick_blocks",
    )(code, rows)


def grid_kernel(order_ref, slot_ref, count_ref, vis_ref, out_ref, wide_ref, acc_ref):
    acc_ref[...] = jnp.zeros_like(acc_ref)
    for piece in range(16):
        wide_ref[piece * WIDE : piece * WIDE + 128, :] = (
            vis_ref[piece * 16 : (piece + 1) * 16].astype(F32).reshape(128, 128)
        )
    cells = lax.broadcasted_iota(jnp.int32, (P_SIZE, 128), 0).astype(F32)
    count = count_ref[0]

    def one_block(at, live):
        entry = order_ref[at]
        slot = slot_ref[at]
        keep = jnp.where(live, 1.0, 0.0).astype(F32)
        first = wide_ref[pl.ds(2 * entry, 16, stride=WIDE), :]
        second = wide_ref[pl.ds(2 * entry + 1, 16, stride=WIDE), :]
        total = None
        for pair in range(4):
            left = []
            right = []
            for k in (2 * pair, 2 * pair + 1):
                real = (first[2 * k : 2 * k + 1] * keep).astype(BF16)
                imag = (second[2 * k : 2 * k + 1] * keep).astype(BF16)
                gap_u = cells - first[2 * k + 1 : 2 * k + 2]
                row = jnp.exp2(gap_u * gap_u * GAUSS).astype(BF16)
                left.append(jnp.concatenate([row * real, row * imag], axis=0))
                gap_v = cells - second[2 * k + 1 : 2 * k + 2]
                right.append(jnp.exp2(gap_v * gap_v * GAUSS).astype(BF16))
            made = nt_dot(
                jnp.concatenate(left, axis=1), jnp.concatenate(right, axis=1)
            )
            total = made if total is None else total + made
        acc_ref[slot] += total.astype(BF16).astype(F32)

    def step(i, carry):
        for t in range(STEP):
            one_block(STEP * i + t, STEP * i + t < count)
        return carry

    lax.fori_loop(0, (count + STEP - 1) // STEP, step, 0)
    for slot in range(BAND * BAND):
        sub_row, sub_col = divmod(slot, BAND)
        for part in range(2):
            for piece in range(4):
                start = part * P_SIZE + piece * 32
                out_ref[
                    4 * sub_row + piece, part, :, sub_col * P_SIZE : (sub_col + 1) * P_SIZE
                ] = acc_ref[slot, start : start + 32, :].astype(BF16)


def grid_blocks(order, slots, count, vis):
    return pl.pallas_call(
        grid_kernel,
        out_shape=jax.ShapeDtypeStruct((16, 2, 32, 512), BF16),
        in_specs=[pl.BlockSpec(memory_space=pltpu.SMEM)] * 3 + [LOCAL],
        out_specs=LOCAL,
        scratch_shapes=[
            pltpu.VMEM((16 * WIDE, 128), F32),
            pltpu.VMEM((BAND * BAND, 2 * P_SIZE, P_SIZE), F32),
        ],
        compiler_params=pltpu.CompilerParams(vmem_limit_bytes=VMEM_LIMIT),
        name="grid_blocks",
    )(order, slots, count, vis)


def add(x, y):
    return x[0] + y[0], x[1] + y[1]


def sub(x, y):
    return x[0] - y[0], x[1] - y[1]


def turn(x):
    return -x[1], x[0]


def scale(x, numer, denom):
    numer %= denom
    if numer == 0:
        return x
    if 4 * numer == denom:
        return turn(x)
    if 2 * numer == denom:
        return -x[0], -x[1]
    if 4 * numer == 3 * denom:
        return x[1], -x[0]
    cosine = float(np.cos(2 * np.pi * numer / denom))
    sine = float(np.sin(2 * np.pi * numer / denom))
    return x[0] * cosine - x[1] * sine, x[0] * sine + x[1] * cosine


def dft4(x0, x1, x2, x3):
    even_sum, even_diff = add(x0, x2), sub(x0, x2)
    odd_sum, odd_diff = add(x1, x3), turn(sub(x1, x3))
    return (
        add(even_sum, odd_sum),
        add(even_diff, odd_diff),
        sub(even_sum, odd_sum),
        sub(even_diff, odd_diff),
    )


def dft16(items):
    firsts = [dft4(*[items[4 * j1 + j2] for j1 in range(4)]) for j2 in range(4)]
    result = [None] * 16
    for b1 in range(4):
        lasts = dft4(*[scale(firsts[j2][b1], j2 * b1, 16) for j2 in range(4)])
        for b2 in range(4):
            result[b1 + 4 * b2] = lasts[b2]
    return result


def row_kernel(
    x_ref, dft_hi_ref, dft_lo_ref, cos_ref, sin_ref, out_ref, mid_ref, hi_ref, lo_ref, put_ref
):
    for half in range(2):
        rows = pl.ds(16 * half, 16)
        for kappa in range(4):
            lanes = pl.ds(128 * kappa, 128)
            items = [
                (x_ref[j, 0, rows, lanes].astype(F32), x_ref[j, 1, rows, lanes].astype(F32))
                for j in range(16)
            ]
            for a1, item in enumerate(dft16(items)):
                item = scale(item, kappa * a1, 64)
                mid_ref[kappa, a1, 0, rows, :] = item[0]
                mid_ref[kappa, a1, 1, rows, :] = item[1]
    for a1 in range(16):
        items = [(mid_ref[kappa, a1, 0], mid_ref[kappa, a1, 1]) for kappa in range(4)]
        for a2, item in enumerate(dft4(*items)):
            a = a1 + 16 * a2
            cosine = cos_ref[a : a + 1, :]
            sine = sin_ref[a : a + 1, :]
            real = item[0] * cosine - item[1] * sine
            imag = item[0] * sine + item[1] * cosine
            both = jnp.concatenate([real, imag], axis=1)
            high, low = split_value(both)
            hi_ref[a * 32 : (a + 1) * 32, :] = high
            lo_ref[a * 32 : (a + 1) * 32, :] = low
    dft_hi = dft_hi_ref[...]
    dft_lo = dft_lo_ref[...]
    for n in range(8):
        high = hi_ref[n * 256 : (n + 1) * 256, :]
        low = lo_ref[n * 256 : (n + 1) * 256, :]
        made = nt_dot(dft_hi, high) + nt_dot(dft_lo, high) + nt_dot(dft_hi, low)
        for part in range(2):
            for piece in range(2):
                half, i = divmod(2 * n + piece, 8)
                put_ref[pl.ds(half * 16 + part * 8 + i, 128, stride=PAD), :] = made[
                    part * 128 : (part + 1) * 128, piece * 128 : (piece + 1) * 128
                ]
    chunks = put_ref[...].reshape(128, PAD, 128)[:, :32]
    out_ref[...] = chunks.reshape(256, 16, 128).astype(BF16)


def row_transform(x):
    tables = [jnp.asarray(t) for t in row_tables()]
    return pl.pallas_call(
        row_kernel,
        out_shape=jax.ShapeDtypeStruct((256, 16, 128), BF16),
        in_specs=[LOCAL] * (1 + len(tables)),
        out_specs=LOCAL,
        scratch_shapes=[
            pltpu.VMEM((4, 16, 2, 32, 128), F32),
            pltpu.VMEM((2048, 256), BF16),
            pltpu.VMEM((2048, 256), BF16),
            pltpu.VMEM((128 * PAD, 128), F32),
        ],
        compiler_params=pltpu.CompilerParams(vmem_limit_bytes=VMEM_LIMIT),
        name="row_transform",
    )(x, *tables)


def column_kernel(
    x_ref, cos_ref, sin_ref, last_hi_ref, last_lo_ref, out_ref, mid_ref, real_ref, imag_ref, put_ref
):
    for chunk in range(16):
        items = []
        for band in range(16):
            value = x_ref[chunk * 16 + band].astype(F32)
            items.append((value[:8], value[8:]))
        for first, item in enumerate(dft16(items)):
            item = scale(item, first * chunk, 256)
            mid_ref[first, chunk, 0] = item[0]
            mid_ref[first, chunk, 1] = item[1]
    for first in range(16):
        items = [(mid_ref[first, chunk, 0], mid_ref[first, chunk, 1]) for chunk in range(16)]
        for second, item in enumerate(dft16(items)):
            at = first + 16 * second
            cosine = cos_ref[at : at + 1, :]
            sine = sin_ref[at : at + 1, :]
            rows = pl.ds(at, 8, stride=GAP)
            real_ref[rows, :] = item[0] * cosine - item[1] * sine
            imag_ref[rows, :] = item[0] * sine + item[1] * cosine
    last_hi = last_hi_ref[...]
    last_lo = last_lo_ref[...]
    for g in range(8):
        both = jnp.concatenate(
            [real_ref[g * GAP : g * GAP + 256, :], imag_ref[g * GAP : g * GAP + 256, :]], axis=1
        )
        high, low = split_value(both)
        made = nt_dot(last_hi, high) + nt_dot(last_lo, high) + nt_dot(last_hi, low)
        for side in range(2):
            for m in range(4):
                start = (side * 32 + 4 * g + m) * PAD
                put_ref[start : start + 32, :] = made[
                    32 * m : 32 * m + 32, side * 128 : (side + 1) * 128
                ]
    for gamma in range(32):
        for side in range(2):
            start = gamma * 256 + side * 128
            out_ref[:, start : start + 128] = put_ref[
                pl.ds(side * 32 * PAD + gamma, 32, stride=PAD), :
            ]


def column_transform(x):
    tables = [jnp.asarray(t) for t in column_tables()]
    return pl.pallas_call(
        column_kernel,
        out_shape=jax.ShapeDtypeStruct((32, N), F32),
        in_specs=[LOCAL] * (1 + len(tables)),
        out_specs=LOCAL,
        scratch_shapes=[
            pltpu.VMEM((16, 16, 2, 8, 128), F32),
            pltpu.VMEM((8 * GAP, 128), F32),
            pltpu.VMEM((8 * GAP, 128), F32),
            pltpu.VMEM((64 * PAD, 128), F32),
        ],
        compiler_params=pltpu.CompilerParams(vmem_limit_bytes=VMEM_LIMIT),
        name="column_transform",
    )(x, *tables)


def block_of(index):
    row = index // SIDE
    col = index % SIDE
    return row // BAND, col // BAND, row % BAND * BAND + col % BAND


def send_code(own_row):
    band, column, slot = block_of(own_row)
    key = column * 16 + band
    number = jnp.arange(own_row.shape[0], dtype=jnp.int32)
    same = (key[None, :] == key[:, None]) & (number[:, None] < number[None, :])
    rank = jnp.sum(same.astype(jnp.int32), axis=0)
    return (key * CAP + rank)[None, :]


def receive_table(sub_index, my_band, my_column):
    band, column, slot = block_of(sub_index)
    inside = (band == my_band) & (column == my_column)
    count = sub_index.shape[1]
    before = (
        jnp.arange(count)[:, None] < jnp.arange(count)[None, :]
    ).astype(BF16)
    rank = jnp.dot(inside.astype(BF16), before, preferred_element_type=F32)
    hit = inside[:, None, :] & (rank[:, None, :] == jnp.arange(CAP, dtype=F32)[None, :, None])
    filled = jnp.any(hit, axis=2).reshape(-1)
    slots = jnp.sum(jnp.where(hit, slot[:, None, :], 0), axis=2).reshape(-1)
    entries = filled.shape[0]
    number = jnp.arange(entries, dtype=jnp.int32)
    place = jnp.sum(
        ((number[None, :] < number[:, None]) & filled[None, :]).astype(jnp.int32), axis=1
    )
    chosen = filled[None, :] & (place[None, :] == number[:, None])
    order = jnp.sum(jnp.where(chosen, number[None, :], 0), axis=1)
    sorted_slots = jnp.sum(jnp.where(chosen, slots[None, :], 0), axis=1)
    total = jnp.sum(filled.astype(jnp.int32)).reshape(1)
    return order, sorted_slots, total


def shards(visibilities, coordinates, phases, sub_index):
    facet_id = lax.axis_index("facet")
    span_id = lax.axis_index("span")
    with jax.named_scope("rotate"):
        parts = rotate_blocks(visibilities[0], coordinates[0], phases[0])
    with jax.named_scope("spread_span"):
        spread = lax.all_to_all(parts, "facet", split_axis=0, concat_axis=0, tiled=True)
    with jax.named_scope("choose"):
        own_row = lax.dynamic_index_in_dim(sub_index, span_id, 0, keepdims=False)
        chosen = pick_blocks(send_code(own_row), spread.reshape(-1, 256))
        order, slots, count = receive_table(sub_index, span_id, facet_id)
    with jax.named_scope("to_owner"):
        arrived = lax.all_to_all(
            chosen, ("facet", "span"), split_axis=0, concat_axis=0, tiled=True
        )
    with jax.named_scope("gridding"):
        block = grid_blocks(order, slots, count, arrived)
    with jax.named_scope("to_rows"):
        rows = lax.all_to_all(block, "facet", split_axis=0, concat_axis=0, tiled=True)
    with jax.named_scope("rows_dft"):
        half_done = row_transform(rows)
    with jax.named_scope("to_columns"):
        columns = lax.all_to_all(
            half_done, ("facet", "span"), split_axis=0, concat_axis=0, tiled=True
        )
    with jax.named_scope("columns_dft"):
        return column_transform(columns)


def solution(mesh):
    return jax.shard_map(
        shards,
        mesh=mesh,
        in_specs=(
            P("span", "facet", None, None),
            P("span", "facet", None, None),
            P("span", "facet", None),
            P(),
        ),
        out_specs=P(("facet", "span"), None),
        check_vma=False,
    )
```

```python
import numpy as np
import jax
import jax.numpy as jnp
from jax import lax
from jax.experimental import pallas as pl
from jax.experimental.pallas import tpu as pltpu
from jax.sharding import PartitionSpec as P

N = 8192
P_SIZE = 128
CAP = 4
STEP = 8
GAP = 264
PAD = 40
WIDE = 136
SIDE = N // P_SIZE
BAND = 4
SPREAD = 0.75
F32 = jnp.float32
BF16 = jnp.bfloat16
GAUSS = -1.0 / (2.0 * SPREAD * SPREAD * np.log(2.0))
VMEM_LIMIT = 24 * 1024 * 1024
LOCAL = pl.BlockSpec(memory_space=pltpu.VMEM)


def angle_tables(rows, cols, length):
    angles = 2.0 * np.pi * ((rows[:, None] * cols[None, :]) % length) / length
    return np.cos(angles), np.sin(angles)


def complex_matrix(cosine, sine):
    return np.block([[cosine, -sine], [sine, cosine]])


def split_table(table):
    high = table.astype(np.float32).astype(BF16)
    low = (table - high.astype(np.float64)).astype(np.float32).astype(BF16)
    return high, low


def row_tables():
    dft_hi, dft_lo = split_table(
        complex_matrix(*angle_tables(np.arange(128), np.arange(128), 128))
    )
    twist_cos, twist_sin = angle_tables(np.arange(64), np.arange(128), N)
    return dft_hi, dft_lo, twist_cos.astype(np.float32), twist_sin.astype(np.float32)


def column_tables():
    lane_r = np.arange(128) % 32
    twist_cos, twist_sin = angle_tables(np.arange(256), lane_r, N)
    cos_r, sin_r = angle_tables(np.arange(32), np.arange(32), 32)
    last = np.concatenate(
        [np.kron(np.eye(4), cos_r), -np.kron(np.eye(4), sin_r)], axis=1
    )
    last_hi, last_lo = split_table(last)
    return (
        (twist_cos / N).astype(np.float32),
        (twist_sin / N).astype(np.float32),
        last_hi,
        last_lo,
    )


def split_value(value):
    high = value.astype(BF16)
    low = (value - high.astype(F32)).astype(BF16)
    return high, low


def nt_dot(left, right):
    return lax.dot_general(
        left, right, (((1,), (1,)), ((), ())), preferred_element_type=F32
    )


def cos_sin(angle):
    half = angle * 0.5
    square = half * half
    sine = jnp.full_like(half, 1.0 / 6227020800.0)
    for coefficient in (-39916800.0, 362880.0, -5040.0, 120.0, -6.0, 1.0):
        sine = sine * square + 1.0 / coefficient
    sine = sine * half
    cosine = jnp.full_like(half, 1.0 / 479001600.0)
    for coefficient in (-3628800.0, 40320.0, -720.0, 24.0, -2.0, 1.0):
        cosine = cosine * square + 1.0 / coefficient
    return 1.0 - 2.0 * sine * sine, 2.0 * sine * cosine


def rotate_kernel(vis_ref, place_ref, phase_ref, out_ref):
    for k in range(8):
        lanes = pl.ds(128 * k, 128)
        cosine, sine = cos_sin(phase_ref[:, lanes])
        real = vis_ref[:, 0, lanes].astype(F32)
        imag = vis_ref[:, 1, lanes].astype(F32)
        out_ref[2 * k, :, :128] = (real * cosine - imag * sine).astype(BF16)
        out_ref[2 * k, :, 128:] = (real * sine + imag * cosine).astype(BF16)
        out_ref[2 * k + 1, :, :128] = place_ref[:, 0, lanes]
        out_ref[2 * k + 1, :, 128:] = place_ref[:, 1, lanes]


def rotate_blocks(visibilities, coordinates, phases):
    blocks = phases.shape[0]
    return pl.pallas_call(
        rotate_kernel,
        out_shape=jax.ShapeDtypeStruct((16, blocks, 256), BF16),
        in_specs=[LOCAL] * 3,
        out_specs=LOCAL,
        name="rotate_blocks",
    )(visibilities, coordinates, phases)


def pick_kernel(code_ref, rows_ref, out_ref, put_ref):
    wanted = lax.broadcasted_iota(jnp.int32, (256, 512), 0)
    for piece in range(4):
        hit = jnp.where(code_ref[...] == wanted + 256 * piece, 1.0, 0.0).astype(BF16)
        for half in range(2):
            made = jnp.dot(
                hit, rows_ref[:, half * 128 : (half + 1) * 128], preferred_element_type=F32
            )
            put_ref[pl.ds(512 * piece + half, 256, stride=2), :] = made
    out_ref[...] = put_ref[...].reshape(256, 8, 128).astype(BF16)


def pick_blocks(code, rows):
    return pl.pallas_call(
        pick_kernel,
        out_shape=jax.ShapeDtypeStruct((256, 8, 128), BF16),
        in_specs=[LOCAL] * 2,
        out_specs=LOCAL,
        scratch_shapes=[pltpu.VMEM((2048, 128), F32)],
        compiler_params=pltpu.CompilerParams(vmem_limit_bytes=VMEM_LIMIT),
        name="pick_blocks",
    )(code, rows)


def grid_kernel(order_ref, slot_ref, count_ref, vis_ref, out_ref, wide_ref, acc_ref):
    acc_ref[...] = jnp.zeros_like(acc_ref)
    for piece in range(16):
        wide_ref[piece * WIDE : piece * WIDE + 128, :] = (
            vis_ref[piece * 16 : (piece + 1) * 16].astype(F32).reshape(128, 128)
        )
    cells = lax.broadcasted_iota(jnp.int32, (P_SIZE, 128), 0).astype(F32)
    count = count_ref[0]

    def blocks_from(start, number, limit):
        places = []
        scales = []
        for t in range(number):
            entry = order_ref[start + t]
            places.append(
                (
                    wide_ref[pl.ds(2 * entry, 16, stride=WIDE), :],
                    wide_ref[pl.ds(2 * entry + 1, 16, stride=WIDE), :],
                )
            )
            live = True if limit is None else start + t < limit
            scales.append(None if limit is None else jnp.where(live, 1.0, 0.0).astype(F32))
        totals = [None] * number
        for pair in range(4):
            for t in range(number):
                first, second = places[t]
                left = []
                right = []
                for k in (2 * pair, 2 * pair + 1):
                    real = first[2 * k : 2 * k + 1]
                    imag = second[2 * k : 2 * k + 1]
                    if scales[t] is not None:
                        real = real * scales[t]
                        imag = imag * scales[t]
                    gap_u = cells - first[2 * k + 1 : 2 * k + 2]
                    row = jnp.exp2(gap_u * gap_u * GAUSS).astype(BF16)
                    left.append(
                        jnp.concatenate([row * real.astype(BF16), row * imag.astype(BF16)], axis=0)
                    )
                    gap_v = cells - second[2 * k + 1 : 2 * k + 2]
                    right.append(jnp.exp2(gap_v * gap_v * GAUSS).astype(BF16))
                made = nt_dot(
                    jnp.concatenate(left, axis=1), jnp.concatenate(right, axis=1)
                )
                totals[t] = made if totals[t] is None else totals[t] + made
        for t in range(number):
            acc_ref[slot_ref[start + t]] += totals[t].astype(BF16).astype(F32)

    def step(i, carry):
        blocks_from(STEP * i, STEP, None)
        return carry

    def last(i, carry):
        blocks_from(2 * i, 2, count)
        return carry

    whole = count // STEP
    lax.fori_loop(0, whole, step, 0)
    lax.fori_loop(whole * (STEP // 2), (count + 1) // 2, last, 0)
    for slot in range(BAND * BAND):
        sub_row, sub_col = divmod(slot, BAND)
        for part in range(2):
            for piece in range(4):
                start = part * P_SIZE + piece * 32
                out_ref[
                    4 * sub_row + piece, part, :, sub_col * P_SIZE : (sub_col + 1) * P_SIZE
                ] = acc_ref[slot, start : start + 32, :].astype(BF16)


def grid_blocks(order, slots, count, vis):
    return pl.pallas_call(
        grid_kernel,
        out_shape=jax.ShapeDtypeStruct((16, 2, 32, 512), BF16),
        in_specs=[pl.BlockSpec(memory_space=pltpu.SMEM)] * 3 + [LOCAL],
        out_specs=LOCAL,
        scratch_shapes=[
            pltpu.VMEM((16 * WIDE, 128), F32),
            pltpu.VMEM((BAND * BAND, 2 * P_SIZE, P_SIZE), F32),
        ],
        compiler_params=pltpu.CompilerParams(vmem_limit_bytes=VMEM_LIMIT),
        name="grid_blocks",
    )(order, slots, count, vis)


def add(x, y):
    return x[0] + y[0], x[1] + y[1]


def sub(x, y):
    return x[0] - y[0], x[1] - y[1]


def turn(x):
    return -x[1], x[0]


def scale(x, numer, denom):
    numer %= denom
    if numer == 0:
        return x
    if 4 * numer == denom:
        return turn(x)
    if 2 * numer == denom:
        return -x[0], -x[1]
    if 4 * numer == 3 * denom:
        return x[1], -x[0]
    cosine = float(np.cos(2 * np.pi * numer / denom))
    sine = float(np.sin(2 * np.pi * numer / denom))
    return x[0] * cosine - x[1] * sine, x[0] * sine + x[1] * cosine


def dft4(x0, x1, x2, x3):
    even_sum, even_diff = add(x0, x2), sub(x0, x2)
    odd_sum, odd_diff = add(x1, x3), turn(sub(x1, x3))
    return (
        add(even_sum, odd_sum),
        add(even_diff, odd_diff),
        sub(even_sum, odd_sum),
        sub(even_diff, odd_diff),
    )


def dft16(items):
    firsts = [dft4(*[items[4 * j1 + j2] for j1 in range(4)]) for j2 in range(4)]
    result = [None] * 16
    for b1 in range(4):
        lasts = dft4(*[scale(firsts[j2][b1], j2 * b1, 16) for j2 in range(4)])
        for b2 in range(4):
            result[b1 + 4 * b2] = lasts[b2]
    return result


def row_kernel(
    x_ref, dft_hi_ref, dft_lo_ref, cos_ref, sin_ref, out_ref, mid_ref, hi_ref, lo_ref, put_ref
):
    for half in range(2):
        rows = pl.ds(16 * half, 16)
        for kappa in range(4):
            lanes = pl.ds(128 * kappa, 128)
            items = [
                (x_ref[j, 0, rows, lanes].astype(F32), x_ref[j, 1, rows, lanes].astype(F32))
                for j in range(16)
            ]
            for a1, item in enumerate(dft16(items)):
                item = scale(item, kappa * a1, 64)
                mid_ref[kappa, a1, 0, rows, :] = item[0]
                mid_ref[kappa, a1, 1, rows, :] = item[1]
    for a1 in range(16):
        items = [(mid_ref[kappa, a1, 0], mid_ref[kappa, a1, 1]) for kappa in range(4)]
        for a2, item in enumerate(dft4(*items)):
            a = a1 + 16 * a2
            cosine = cos_ref[a : a + 1, :]
            sine = sin_ref[a : a + 1, :]
            real = item[0] * cosine - item[1] * sine
            imag = item[0] * sine + item[1] * cosine
            both = jnp.concatenate([real, imag], axis=1)
            high, low = split_value(both)
            hi_ref[a * 32 : (a + 1) * 32, :] = high
            lo_ref[a * 32 : (a + 1) * 32, :] = low
    dft_hi = dft_hi_ref[...]
    dft_lo = dft_lo_ref[...]
    for n in range(8):
        high = hi_ref[n * 256 : (n + 1) * 256, :]
        low = lo_ref[n * 256 : (n + 1) * 256, :]
        made = nt_dot(dft_hi, high) + nt_dot(dft_lo, high) + nt_dot(dft_hi, low)
        for part in range(2):
            for piece in range(2):
                half, i = divmod(2 * n + piece, 8)
                put_ref[pl.ds(half * 16 + part * 8 + i, 128, stride=PAD), :] = made[
                    part * 128 : (part + 1) * 128, piece * 128 : (piece + 1) * 128
                ]
    chunks = put_ref[...].reshape(128, PAD, 128)[:, :32]
    out_ref[...] = chunks.reshape(256, 16, 128).astype(BF16)


def row_transform(x):
    tables = [jnp.asarray(t) for t in row_tables()]
    return pl.pallas_call(
        row_kernel,
        out_shape=jax.ShapeDtypeStruct((256, 16, 128), BF16),
        in_specs=[LOCAL] * (1 + len(tables)),
        out_specs=LOCAL,
        scratch_shapes=[
            pltpu.VMEM((4, 16, 2, 32, 128), F32),
            pltpu.VMEM((2048, 256), BF16),
            pltpu.VMEM((2048, 256), BF16),
            pltpu.VMEM((128 * PAD, 128), F32),
        ],
        compiler_params=pltpu.CompilerParams(vmem_limit_bytes=VMEM_LIMIT),
        name="row_transform",
    )(x, *tables)


def column_kernel(
    x_ref, cos_ref, sin_ref, last_hi_ref, last_lo_ref, out_ref, mid_ref, real_ref, imag_ref, put_ref
):
    for chunk in range(16):
        items = []
        for band in range(16):
            value = x_ref[chunk * 16 + band].astype(F32)
            items.append((value[:8], value[8:]))
        for first, item in enumerate(dft16(items)):
            item = scale(item, first * chunk, 256)
            mid_ref[first, chunk, 0] = item[0]
            mid_ref[first, chunk, 1] = item[1]
    for first in range(16):
        items = [(mid_ref[first, chunk, 0], mid_ref[first, chunk, 1]) for chunk in range(16)]
        for second, item in enumerate(dft16(items)):
            at = first + 16 * second
            cosine = cos_ref[at : at + 1, :]
            sine = sin_ref[at : at + 1, :]
            rows = pl.ds(at, 8, stride=GAP)
            real_ref[rows, :] = item[0] * cosine - item[1] * sine
            imag_ref[rows, :] = item[0] * sine + item[1] * cosine
    last_hi = last_hi_ref[...]
    last_lo = last_lo_ref[...]
    for g in range(8):
        both = jnp.concatenate(
            [real_ref[g * GAP : g * GAP + 256, :], imag_ref[g * GAP : g * GAP + 256, :]], axis=1
        )
        high, low = split_value(both)
        made = nt_dot(last_hi, high) + nt_dot(last_lo, high) + nt_dot(last_hi, low)
        for side in range(2):
            for m in range(4):
                start = (side * 32 + 4 * g + m) * PAD
                put_ref[start : start + 32, :] = made[
                    32 * m : 32 * m + 32, side * 128 : (side + 1) * 128
                ]
    for gamma in range(32):
        for side in range(2):
            start = gamma * 256 + side * 128
            out_ref[:, start : start + 128] = put_ref[
                pl.ds(side * 32 * PAD + gamma, 32, stride=PAD), :
            ]


def column_transform(x):
    tables = [jnp.asarray(t) for t in column_tables()]
    return pl.pallas_call(
        column_kernel,
        out_shape=jax.ShapeDtypeStruct((32, N), F32),
        in_specs=[LOCAL] * (1 + len(tables)),
        out_specs=LOCAL,
        scratch_shapes=[
            pltpu.VMEM((16, 16, 2, 8, 128), F32),
            pltpu.VMEM((8 * GAP, 128), F32),
            pltpu.VMEM((8 * GAP, 128), F32),
            pltpu.VMEM((64 * PAD, 128), F32),
        ],
        compiler_params=pltpu.CompilerParams(vmem_limit_bytes=VMEM_LIMIT),
        name="column_transform",
    )(x, *tables)


def block_of(index):
    row = index // SIDE
    col = index % SIDE
    return row // BAND, col // BAND, row % BAND * BAND + col % BAND


def send_code(own_row):
    band, column, slot = block_of(own_row)
    key = column * 16 + band
    number = jnp.arange(own_row.shape[0], dtype=jnp.int32)
    same = (key[None, :] == key[:, None]) & (number[:, None] < number[None, :])
    rank = jnp.sum(same.astype(jnp.int32), axis=0)
    return (key * CAP + rank)[None, :]


def receive_table(sub_index, my_band, my_column):
    band, column, slot = block_of(sub_index)
    inside = (band == my_band) & (column == my_column)
    count = sub_index.shape[1]
    before = (
        jnp.arange(count)[:, None] < jnp.arange(count)[None, :]
    ).astype(BF16)
    rank = jnp.dot(inside.astype(BF16), before, preferred_element_type=F32)
    hit = inside[:, None, :] & (rank[:, None, :] == jnp.arange(CAP, dtype=F32)[None, :, None])
    filled = jnp.any(hit, axis=2).reshape(-1)
    slots = jnp.sum(jnp.where(hit, slot[:, None, :], 0), axis=2).reshape(-1)
    entries = filled.shape[0]
    number = jnp.arange(entries, dtype=jnp.int32)
    place = jnp.sum(
        ((number[None, :] < number[:, None]) & filled[None, :]).astype(jnp.int32), axis=1
    )
    chosen = filled[None, :] & (place[None, :] == number[:, None])
    order = jnp.sum(jnp.where(chosen, number[None, :], 0), axis=1)
    sorted_slots = jnp.sum(jnp.where(chosen, slots[None, :], 0), axis=1)
    total = jnp.sum(filled.astype(jnp.int32)).reshape(1)
    return order, sorted_slots, total


def shards(visibilities, coordinates, phases, sub_index):
    facet_id = lax.axis_index("facet")
    span_id = lax.axis_index("span")
    with jax.named_scope("rotate"):
        parts = rotate_blocks(visibilities[0], coordinates[0], phases[0])
    with jax.named_scope("spread_span"):
        spread = lax.all_to_all(parts, "facet", split_axis=0, concat_axis=0, tiled=True)
    with jax.named_scope("choose"):
        own_row = lax.dynamic_index_in_dim(sub_index, span_id, 0, keepdims=False)
        order, slots, count = receive_table(sub_index, span_id, facet_id)
        spread, order, slots, count = lax.optimization_barrier((spread, order, slots, count))
        chosen = pick_blocks(send_code(own_row), spread.reshape(-1, 256))
    with jax.named_scope("to_owner"):
        arrived = lax.all_to_all(
            chosen, ("facet", "span"), split_axis=0, concat_axis=0, tiled=True
        )
    with jax.named_scope("gridding"):
        block = grid_blocks(order, slots, count, arrived)
    with jax.named_scope("to_rows"):
        rows = lax.all_to_all(block, "facet", split_axis=0, concat_axis=0, tiled=True)
    with jax.named_scope("rows_dft"):
        half_done = row_transform(rows)
    with jax.named_scope("to_columns"):
        columns = lax.all_to_all(
            half_done, ("facet", "span"), split_axis=0, concat_axis=0, tiled=True
        )
    with jax.named_scope("columns_dft"):
        return column_transform(columns)


def solution(mesh):
    return jax.shard_map(
        shards,
        mesh=mesh,
        in_specs=(
            P("span", "facet", None, None),
            P("span", "facet", None, None),
            P("span", "facet", None),
            P(),
        ),
        out_specs=P(("facet", "span"), None),
        check_vma=False,
    )
```

```python
import numpy as np
import jax
import jax.numpy as jnp
from jax import lax
from jax.experimental import pallas as pl
from jax.experimental.pallas import tpu as pltpu
from jax.sharding import PartitionSpec as P

N = 8192
P_SIZE = 128
CAP = 4
STEP = 8
GAP = 264
PAD = 40
WIDE = 136
SIDE = N // P_SIZE
BAND = 4
SPREAD = 0.75
F32 = jnp.float32
BF16 = jnp.bfloat16
GAUSS = -1.0 / (2.0 * SPREAD * SPREAD * np.log(2.0))
VMEM_LIMIT = 24 * 1024 * 1024
LOCAL = pl.BlockSpec(memory_space=pltpu.VMEM)


def angle_tables(rows, cols, length):
    angles = 2.0 * np.pi * ((rows[:, None] * cols[None, :]) % length) / length
    return np.cos(angles), np.sin(angles)


def complex_matrix(cosine, sine):
    return np.block([[cosine, -sine], [sine, cosine]])


def split_table(table):
    high = table.astype(np.float32).astype(BF16)
    low = (table - high.astype(np.float64)).astype(np.float32).astype(BF16)
    return high, low


def row_tables():
    dft_hi, dft_lo = split_table(
        complex_matrix(*angle_tables(np.arange(128), np.arange(128), 128))
    )
    twist_cos, twist_sin = angle_tables(np.arange(64), np.arange(128), N)
    return dft_hi, dft_lo, twist_cos.astype(np.float32), twist_sin.astype(np.float32)


def column_tables():
    lane_r = np.arange(128) % 32
    twist_cos, twist_sin = angle_tables(np.arange(256), lane_r, N)
    cos_r, sin_r = angle_tables(np.arange(32), np.arange(32), 32)
    last = np.concatenate(
        [np.kron(np.eye(4), cos_r), -np.kron(np.eye(4), sin_r)], axis=1
    )
    last_hi, _ = split_table(last)
    return (
        (twist_cos / N).astype(np.float32),
        (twist_sin / N).astype(np.float32),
        last_hi,
    )


def split_value(value):
    high = value.astype(BF16)
    low = (value - high.astype(F32)).astype(BF16)
    return high, low


def nt_dot(left, right):
    return lax.dot_general(
        left, right, (((1,), (1,)), ((), ())), preferred_element_type=F32
    )


def cos_sin(angle):
    half = angle * 0.5
    square = half * half
    sine = jnp.full_like(half, 1.0 / 6227020800.0)
    for coefficient in (-39916800.0, 362880.0, -5040.0, 120.0, -6.0, 1.0):
        sine = sine * square + 1.0 / coefficient
    sine = sine * half
    cosine = jnp.full_like(half, 1.0 / 479001600.0)
    for coefficient in (-3628800.0, 40320.0, -720.0, 24.0, -2.0, 1.0):
        cosine = cosine * square + 1.0 / coefficient
    return 1.0 - 2.0 * sine * sine, 2.0 * sine * cosine


def rotate_kernel(vis_ref, place_ref, phase_ref, out_ref):
    for k in range(8):
        lanes = pl.ds(128 * k, 128)
        cosine, sine = cos_sin(phase_ref[:, lanes])
        real = vis_ref[:, 0, lanes].astype(F32)
        imag = vis_ref[:, 1, lanes].astype(F32)
        out_ref[2 * k, :, :128] = (real * cosine - imag * sine).astype(BF16)
        out_ref[2 * k, :, 128:] = (real * sine + imag * cosine).astype(BF16)
        out_ref[2 * k + 1, :, :128] = place_ref[:, 0, lanes]
        out_ref[2 * k + 1, :, 128:] = place_ref[:, 1, lanes]


def rotate_blocks(visibilities, coordinates, phases):
    blocks = phases.shape[0]
    return pl.pallas_call(
        rotate_kernel,
        out_shape=jax.ShapeDtypeStruct((16, blocks, 256), BF16),
        in_specs=[LOCAL] * 3,
        out_specs=LOCAL,
        name="rotate_blocks",
    )(visibilities, coordinates, phases)


def pick_kernel(code_ref, rows_ref, out_ref, put_ref):
    wanted = lax.broadcasted_iota(jnp.int32, (256, 512), 0)
    for piece in range(4):
        hit = jnp.where(code_ref[...] == wanted + 256 * piece, 1.0, 0.0).astype(BF16)
        for half in range(2):
            made = jnp.dot(
                hit, rows_ref[:, half * 128 : (half + 1) * 128], preferred_element_type=F32
            )
            put_ref[pl.ds(512 * piece + half, 256, stride=2), :] = made
    out_ref[...] = put_ref[...].reshape(256, 8, 128).astype(BF16)


def pick_blocks(code, rows):
    return pl.pallas_call(
        pick_kernel,
        out_shape=jax.ShapeDtypeStruct((256, 8, 128), BF16),
        in_specs=[LOCAL] * 2,
        out_specs=LOCAL,
        scratch_shapes=[pltpu.VMEM((2048, 128), F32)],
        compiler_params=pltpu.CompilerParams(vmem_limit_bytes=VMEM_LIMIT),
        name="pick_blocks",
    )(code, rows)


def grid_kernel(order_ref, slot_ref, count_ref, vis_ref, out_ref, wide_ref, acc_ref):
    acc_ref[...] = jnp.zeros_like(acc_ref)
    for piece in range(16):
        wide_ref[piece * WIDE : piece * WIDE + 128, :] = (
            vis_ref[piece * 16 : (piece + 1) * 16].astype(F32).reshape(128, 128)
        )
    cells = lax.broadcasted_iota(jnp.int32, (P_SIZE, 128), 0).astype(F32)
    count = count_ref[0]

    def blocks_from(start, number, limit):
        places = []
        scales = []
        for t in range(number):
            entry = order_ref[start + t]
            places.append(
                (
                    wide_ref[pl.ds(2 * entry, 16, stride=WIDE), :],
                    wide_ref[pl.ds(2 * entry + 1, 16, stride=WIDE), :],
                )
            )
            live = True if limit is None else start + t < limit
            scales.append(None if limit is None else jnp.where(live, 1.0, 0.0).astype(F32))
        totals = [None] * number
        for pair in range(4):
            for t in range(number):
                first, second = places[t]
                left = []
                right = []
                for k in (2 * pair, 2 * pair + 1):
                    real = first[2 * k : 2 * k + 1]
                    imag = second[2 * k : 2 * k + 1]
                    if scales[t] is not None:
                        real = real * scales[t]
                        imag = imag * scales[t]
                    gap_u = cells - first[2 * k + 1 : 2 * k + 2]
                    row = jnp.exp2(gap_u * gap_u * GAUSS).astype(BF16)
                    left.append(
                        jnp.concatenate([row * real.astype(BF16), row * imag.astype(BF16)], axis=0)
                    )
                    gap_v = cells - second[2 * k + 1 : 2 * k + 2]
                    right.append(jnp.exp2(gap_v * gap_v * GAUSS).astype(BF16))
                made = nt_dot(
                    jnp.concatenate(left, axis=1), jnp.concatenate(right, axis=1)
                )
                totals[t] = made if totals[t] is None else totals[t] + made
        for t in range(number):
            acc_ref[slot_ref[start + t]] += totals[t].astype(BF16).astype(F32)

    def step(i, carry):
        blocks_from(STEP * i, STEP, None)
        return carry

    def last(i, carry):
        blocks_from(2 * i, 2, count)
        return carry

    whole = count // STEP
    lax.fori_loop(0, whole, step, 0)
    lax.fori_loop(whole * (STEP // 2), (count + 1) // 2, last, 0)
    for slot in range(BAND * BAND):
        sub_row, sub_col = divmod(slot, BAND)
        for part in range(2):
            for piece in range(4):
                start = part * P_SIZE + piece * 32
                out_ref[
                    4 * sub_row + piece, part, :, sub_col * P_SIZE : (sub_col + 1) * P_SIZE
                ] = acc_ref[slot, start : start + 32, :].astype(BF16)


def grid_blocks(order, slots, count, vis):
    return pl.pallas_call(
        grid_kernel,
        out_shape=jax.ShapeDtypeStruct((16, 2, 32, 512), BF16),
        in_specs=[pl.BlockSpec(memory_space=pltpu.SMEM)] * 3 + [LOCAL],
        out_specs=LOCAL,
        scratch_shapes=[
            pltpu.VMEM((16 * WIDE, 128), F32),
            pltpu.VMEM((BAND * BAND, 2 * P_SIZE, P_SIZE), F32),
        ],
        compiler_params=pltpu.CompilerParams(vmem_limit_bytes=VMEM_LIMIT),
        name="grid_blocks",
    )(order, slots, count, vis)


def add(x, y):
    return x[0] + y[0], x[1] + y[1]


def sub(x, y):
    return x[0] - y[0], x[1] - y[1]


def turn(x):
    return -x[1], x[0]


def scale(x, numer, denom):
    numer %= denom
    if numer == 0:
        return x
    if 4 * numer == denom:
        return turn(x)
    if 2 * numer == denom:
        return -x[0], -x[1]
    if 4 * numer == 3 * denom:
        return x[1], -x[0]
    cosine = float(np.cos(2 * np.pi * numer / denom))
    sine = float(np.sin(2 * np.pi * numer / denom))
    return x[0] * cosine - x[1] * sine, x[0] * sine + x[1] * cosine


def dft4(x0, x1, x2, x3):
    even_sum, even_diff = add(x0, x2), sub(x0, x2)
    odd_sum, odd_diff = add(x1, x3), turn(sub(x1, x3))
    return (
        add(even_sum, odd_sum),
        add(even_diff, odd_diff),
        sub(even_sum, odd_sum),
        sub(even_diff, odd_diff),
    )


def dft16(items):
    firsts = [dft4(*[items[4 * j1 + j2] for j1 in range(4)]) for j2 in range(4)]
    result = [None] * 16
    for b1 in range(4):
        lasts = dft4(*[scale(firsts[j2][b1], j2 * b1, 16) for j2 in range(4)])
        for b2 in range(4):
            result[b1 + 4 * b2] = lasts[b2]
    return result


def row_kernel(
    x_ref, dft_hi_ref, dft_lo_ref, cos_ref, sin_ref, out_ref, mid_ref, hi_ref, lo_ref, put_ref
):
    for half in range(2):
        rows = pl.ds(16 * half, 16)
        for kappa in range(4):
            lanes = pl.ds(128 * kappa, 128)
            items = [
                (x_ref[j, 0, rows, lanes].astype(F32), x_ref[j, 1, rows, lanes].astype(F32))
                for j in range(16)
            ]
            for a1, item in enumerate(dft16(items)):
                item = scale(item, kappa * a1, 64)
                mid_ref[kappa, a1, 0, rows, :] = item[0]
                mid_ref[kappa, a1, 1, rows, :] = item[1]
    for a1 in range(16):
        items = [(mid_ref[kappa, a1, 0], mid_ref[kappa, a1, 1]) for kappa in range(4)]
        for a2, item in enumerate(dft4(*items)):
            a = a1 + 16 * a2
            cosine = cos_ref[a : a + 1, :]
            sine = sin_ref[a : a + 1, :]
            real = item[0] * cosine - item[1] * sine
            imag = item[0] * sine + item[1] * cosine
            both = jnp.concatenate([real, imag], axis=1)
            high, low = split_value(both)
            hi_ref[a * 32 : (a + 1) * 32, :] = high
            lo_ref[a * 32 : (a + 1) * 32, :] = low
    dft_hi = dft_hi_ref[...]
    dft_lo = dft_lo_ref[...]
    for n in range(8):
        high = hi_ref[n * 256 : (n + 1) * 256, :]
        low = lo_ref[n * 256 : (n + 1) * 256, :]
        made = nt_dot(dft_hi, high) + nt_dot(dft_lo, high) + nt_dot(dft_hi, low)
        for part in range(2):
            for piece in range(2):
                half, i = divmod(2 * n + piece, 8)
                put_ref[pl.ds(half * 16 + part * 8 + i, 128, stride=PAD), :] = made[
                    part * 128 : (part + 1) * 128, piece * 128 : (piece + 1) * 128
                ]
    chunks = put_ref[...].reshape(128, PAD, 128)[:, :32]
    out_ref[...] = chunks.reshape(256, 16, 128).astype(BF16)


def row_transform(x):
    tables = [jnp.asarray(t) for t in row_tables()]
    return pl.pallas_call(
        row_kernel,
        out_shape=jax.ShapeDtypeStruct((256, 16, 128), BF16),
        in_specs=[LOCAL] * (1 + len(tables)),
        out_specs=LOCAL,
        scratch_shapes=[
            pltpu.VMEM((4, 16, 2, 32, 128), F32),
            pltpu.VMEM((2048, 256), BF16),
            pltpu.VMEM((2048, 256), BF16),
            pltpu.VMEM((128 * PAD, 128), F32),
        ],
        compiler_params=pltpu.CompilerParams(vmem_limit_bytes=VMEM_LIMIT),
        name="row_transform",
    )(x, *tables)


def column_kernel(
    x_ref, cos_ref, sin_ref, last_hi_ref, out_ref, mid_ref, real_ref, imag_ref, put_ref
):
    for chunk in range(16):
        items = []
        for band in range(16):
            value = x_ref[chunk * 16 + band].astype(F32)
            items.append((value[:8], value[8:]))
        for first, item in enumerate(dft16(items)):
            item = scale(item, first * chunk, 256)
            mid_ref[first, chunk, 0] = item[0]
            mid_ref[first, chunk, 1] = item[1]
    for first in range(16):
        items = [(mid_ref[first, chunk, 0], mid_ref[first, chunk, 1]) for chunk in range(16)]
        for second, item in enumerate(dft16(items)):
            at = first + 16 * second
            cosine = cos_ref[at : at + 1, :]
            sine = sin_ref[at : at + 1, :]
            rows = pl.ds(at, 8, stride=GAP)
            real_ref[rows, :] = item[0] * cosine - item[1] * sine
            imag_ref[rows, :] = item[0] * sine + item[1] * cosine
    last_hi = last_hi_ref[...]
    for g in range(8):
        both = jnp.concatenate(
            [real_ref[g * GAP : g * GAP + 256, :], imag_ref[g * GAP : g * GAP + 256, :]], axis=1
        )
        high, low = split_value(both)
        made = nt_dot(last_hi, high) + nt_dot(last_hi, low)
        for side in range(2):
            for m in range(4):
                start = (side * 32 + 4 * g + m) * PAD
                put_ref[start : start + 32, :] = made[
                    32 * m : 32 * m + 32, side * 128 : (side + 1) * 128
                ]
    for gamma in range(32):
        for side in range(2):
            start = gamma * 256 + side * 128
            out_ref[:, start : start + 128] = put_ref[
                pl.ds(side * 32 * PAD + gamma, 32, stride=PAD), :
            ]


def column_transform(x):
    tables = [jnp.asarray(t) for t in column_tables()]
    return pl.pallas_call(
        column_kernel,
        out_shape=jax.ShapeDtypeStruct((32, N), F32),
        in_specs=[LOCAL] * (1 + len(tables)),
        out_specs=LOCAL,
        scratch_shapes=[
            pltpu.VMEM((16, 16, 2, 8, 128), F32),
            pltpu.VMEM((8 * GAP, 128), F32),
            pltpu.VMEM((8 * GAP, 128), F32),
            pltpu.VMEM((64 * PAD, 128), F32),
        ],
        compiler_params=pltpu.CompilerParams(vmem_limit_bytes=VMEM_LIMIT),
        name="column_transform",
    )(x, *tables)


def block_of(index):
    row = index // SIDE
    col = index % SIDE
    return row // BAND, col // BAND, row % BAND * BAND + col % BAND


def send_code(own_row):
    band, column, slot = block_of(own_row)
    key = column * 16 + band
    number = jnp.arange(own_row.shape[0], dtype=jnp.int32)
    same = (key[None, :] == key[:, None]) & (number[:, None] < number[None, :])
    rank = jnp.sum(same.astype(jnp.int32), axis=0)
    return (key * CAP + rank)[None, :]


def receive_table(sub_index, my_band, my_column):
    band, column, slot = block_of(sub_index)
    inside = (band == my_band) & (column == my_column)
    count = sub_index.shape[1]
    before = (
        jnp.arange(count)[:, None] < jnp.arange(count)[None, :]
    ).astype(BF16)
    rank = jnp.dot(inside.astype(BF16), before, preferred_element_type=F32)
    hit = inside[:, None, :] & (rank[:, None, :] == jnp.arange(CAP, dtype=F32)[None, :, None])
    filled = jnp.any(hit, axis=2).reshape(-1)
    slots = jnp.sum(jnp.where(hit, slot[:, None, :], 0), axis=2).reshape(-1)
    entries = filled.shape[0]
    number = jnp.arange(entries, dtype=jnp.int32)
    place = jnp.sum(
        ((number[None, :] < number[:, None]) & filled[None, :]).astype(jnp.int32), axis=1
    )
    chosen = filled[None, :] & (place[None, :] == number[:, None])
    order = jnp.sum(jnp.where(chosen, number[None, :], 0), axis=1)
    sorted_slots = jnp.sum(jnp.where(chosen, slots[None, :], 0), axis=1)
    total = jnp.sum(filled.astype(jnp.int32)).reshape(1)
    return order, sorted_slots, total


def shards(visibilities, coordinates, phases, sub_index):
    facet_id = lax.axis_index("facet")
    span_id = lax.axis_index("span")
    with jax.named_scope("rotate"):
        parts = rotate_blocks(visibilities[0], coordinates[0], phases[0])
    with jax.named_scope("spread_span"):
        spread = lax.all_to_all(parts, "facet", split_axis=0, concat_axis=0, tiled=True)
    with jax.named_scope("choose"):
        own_row = lax.dynamic_index_in_dim(sub_index, span_id, 0, keepdims=False)
        order, slots, count = receive_table(sub_index, span_id, facet_id)
        spread, order, slots, count = lax.optimization_barrier((spread, order, slots, count))
        chosen = pick_blocks(send_code(own_row), spread.reshape(-1, 256))
    with jax.named_scope("to_owner"):
        arrived = lax.all_to_all(
            chosen, ("facet", "span"), split_axis=0, concat_axis=0, tiled=True
        )
    with jax.named_scope("gridding"):
        block = grid_blocks(order, slots, count, arrived)
    with jax.named_scope("to_rows"):
        rows = lax.all_to_all(block, "facet", split_axis=0, concat_axis=0, tiled=True)
    with jax.named_scope("rows_dft"):
        half_done = row_transform(rows)
    with jax.named_scope("to_columns"):
        columns = lax.all_to_all(
            half_done, ("facet", "span"), split_axis=0, concat_axis=0, tiled=True
        )
    with jax.named_scope("columns_dft"):
        return column_transform(columns)


def solution(mesh):
    return jax.shard_map(
        shards,
        mesh=mesh,
        in_specs=(
            P("span", "facet", None, None),
            P("span", "facet", None, None),
            P("span", "facet", None),
            P(),
        ),
        out_specs=P(("facet", "span"), None),
        check_vma=False,
    )
```

```python
import numpy as np
import jax
import jax.numpy as jnp
from jax import lax
from jax.experimental import pallas as pl
from jax.experimental.pallas import tpu as pltpu
from jax.sharding import PartitionSpec as P

N = 8192
P_SIZE = 128
CAP = 4
STEP = 8
GAP = 264
PAD = 40
WIDE = 136
SIDE = N // P_SIZE
BAND = 4
SPREAD = 0.75
F32 = jnp.float32
BF16 = jnp.bfloat16
GAUSS = -1.0 / (2.0 * SPREAD * SPREAD * np.log(2.0))
VMEM_LIMIT = 24 * 1024 * 1024
LOCAL = pl.BlockSpec(memory_space=pltpu.VMEM)


def angle_tables(rows, cols, length):
    angles = 2.0 * np.pi * ((rows[:, None] * cols[None, :]) % length) / length
    return np.cos(angles), np.sin(angles)


def complex_matrix(cosine, sine):
    return np.block([[cosine, -sine], [sine, cosine]])


def split_table(table):
    high = table.astype(np.float32).astype(BF16)
    low = (table - high.astype(np.float64)).astype(np.float32).astype(BF16)
    return high, low


def row_tables():
    dft_hi, _ = split_table(
        complex_matrix(*angle_tables(np.arange(128), np.arange(128), 128))
    )
    twist_cos, twist_sin = angle_tables(np.arange(64), np.arange(128), N)
    return dft_hi, twist_cos.astype(np.float32), twist_sin.astype(np.float32)


def column_tables():
    lane_r = np.arange(128) % 32
    twist_cos, twist_sin = angle_tables(np.arange(256), lane_r, N)
    cos_r, sin_r = angle_tables(np.arange(32), np.arange(32), 32)
    last = np.concatenate(
        [np.kron(np.eye(4), cos_r), -np.kron(np.eye(4), sin_r)], axis=1
    )
    last_hi, _ = split_table(last)
    return (
        (twist_cos / N).astype(np.float32),
        (twist_sin / N).astype(np.float32),
        last_hi,
    )


def split_value(value):
    high = value.astype(BF16)
    low = (value - high.astype(F32)).astype(BF16)
    return high, low


def nt_dot(left, right):
    return lax.dot_general(
        left, right, (((1,), (1,)), ((), ())), preferred_element_type=F32
    )


def cos_sin(angle):
    half = angle * 0.5
    square = half * half
    sine = jnp.full_like(half, 1.0 / 6227020800.0)
    for coefficient in (-39916800.0, 362880.0, -5040.0, 120.0, -6.0, 1.0):
        sine = sine * square + 1.0 / coefficient
    sine = sine * half
    cosine = jnp.full_like(half, 1.0 / 479001600.0)
    for coefficient in (-3628800.0, 40320.0, -720.0, 24.0, -2.0, 1.0):
        cosine = cosine * square + 1.0 / coefficient
    return 1.0 - 2.0 * sine * sine, 2.0 * sine * cosine


def rotate_kernel(vis_ref, place_ref, phase_ref, out_ref):
    for k in range(8):
        lanes = pl.ds(128 * k, 128)
        cosine, sine = cos_sin(phase_ref[:, lanes])
        real = vis_ref[:, 0, lanes].astype(F32)
        imag = vis_ref[:, 1, lanes].astype(F32)
        out_ref[2 * k, :, :128] = (real * cosine - imag * sine).astype(BF16)
        out_ref[2 * k, :, 128:] = (real * sine + imag * cosine).astype(BF16)
        out_ref[2 * k + 1, :, :128] = place_ref[:, 0, lanes]
        out_ref[2 * k + 1, :, 128:] = place_ref[:, 1, lanes]


def rotate_blocks(visibilities, coordinates, phases):
    blocks = phases.shape[0]
    return pl.pallas_call(
        rotate_kernel,
        out_shape=jax.ShapeDtypeStruct((16, blocks, 256), BF16),
        in_specs=[LOCAL] * 3,
        out_specs=LOCAL,
        name="rotate_blocks",
    )(visibilities, coordinates, phases)


def pick_kernel(code_ref, rows_ref, out_ref, put_ref):
    wanted = lax.broadcasted_iota(jnp.int32, (256, 512), 0)
    for piece in range(4):
        hit = jnp.where(code_ref[...] == wanted + 256 * piece, 1.0, 0.0).astype(BF16)
        for half in range(2):
            made = jnp.dot(
                hit, rows_ref[:, half * 128 : (half + 1) * 128], preferred_element_type=F32
            )
            put_ref[pl.ds(512 * piece + half, 256, stride=2), :] = made
    out_ref[...] = put_ref[...].reshape(256, 8, 128).astype(BF16)


def pick_blocks(code, rows):
    return pl.pallas_call(
        pick_kernel,
        out_shape=jax.ShapeDtypeStruct((256, 8, 128), BF16),
        in_specs=[LOCAL] * 2,
        out_specs=LOCAL,
        scratch_shapes=[pltpu.VMEM((2048, 128), F32)],
        compiler_params=pltpu.CompilerParams(vmem_limit_bytes=VMEM_LIMIT),
        name="pick_blocks",
    )(code, rows)


def grid_kernel(order_ref, slot_ref, count_ref, vis_ref, out_ref, wide_ref, acc_ref):
    acc_ref[...] = jnp.zeros_like(acc_ref)
    for piece in range(16):
        wide_ref[piece * WIDE : piece * WIDE + 128, :] = (
            vis_ref[piece * 16 : (piece + 1) * 16].astype(F32).reshape(128, 128)
        )
    cells = lax.broadcasted_iota(jnp.int32, (P_SIZE, 128), 0).astype(F32)
    count = count_ref[0]

    def blocks_from(start, number, limit):
        places = []
        scales = []
        for t in range(number):
            entry = order_ref[start + t]
            places.append(
                (
                    wide_ref[pl.ds(2 * entry, 16, stride=WIDE), :],
                    wide_ref[pl.ds(2 * entry + 1, 16, stride=WIDE), :],
                )
            )
            live = True if limit is None else start + t < limit
            scales.append(None if limit is None else jnp.where(live, 1.0, 0.0).astype(F32))
        totals = [None] * number
        for pair in range(4):
            for t in range(number):
                first, second = places[t]
                left = []
                right = []
                for k in (2 * pair, 2 * pair + 1):
                    real = first[2 * k : 2 * k + 1]
                    imag = second[2 * k : 2 * k + 1]
                    if scales[t] is not None:
                        real = real * scales[t]
                        imag = imag * scales[t]
                    gap_u = cells - first[2 * k + 1 : 2 * k + 2]
                    row = jnp.exp2(gap_u * gap_u * GAUSS).astype(BF16)
                    left.append(
                        jnp.concatenate([row * real.astype(BF16), row * imag.astype(BF16)], axis=0)
                    )
                    gap_v = cells - second[2 * k + 1 : 2 * k + 2]
                    right.append(jnp.exp2(gap_v * gap_v * GAUSS).astype(BF16))
                made = nt_dot(
                    jnp.concatenate(left, axis=1), jnp.concatenate(right, axis=1)
                )
                totals[t] = made if totals[t] is None else totals[t] + made
        for t in range(number):
            acc_ref[slot_ref[start + t]] += totals[t].astype(BF16).astype(F32)

    def step(i, carry):
        blocks_from(STEP * i, STEP, None)
        return carry

    def last(i, carry):
        blocks_from(2 * i, 2, count)
        return carry

    whole = count // STEP
    lax.fori_loop(0, whole, step, 0)
    lax.fori_loop(whole * (STEP // 2), (count + 1) // 2, last, 0)
    for slot in range(BAND * BAND):
        sub_row, sub_col = divmod(slot, BAND)
        for part in range(2):
            for piece in range(4):
                start = part * P_SIZE + piece * 32
                out_ref[
                    4 * sub_row + piece, part, :, sub_col * P_SIZE : (sub_col + 1) * P_SIZE
                ] = acc_ref[slot, start : start + 32, :].astype(BF16)


def grid_blocks(order, slots, count, vis):
    return pl.pallas_call(
        grid_kernel,
        out_shape=jax.ShapeDtypeStruct((16, 2, 32, 512), BF16),
        in_specs=[pl.BlockSpec(memory_space=pltpu.SMEM)] * 3 + [LOCAL],
        out_specs=LOCAL,
        scratch_shapes=[
            pltpu.VMEM((16 * WIDE, 128), F32),
            pltpu.VMEM((BAND * BAND, 2 * P_SIZE, P_SIZE), F32),
        ],
        compiler_params=pltpu.CompilerParams(vmem_limit_bytes=VMEM_LIMIT),
        name="grid_blocks",
    )(order, slots, count, vis)


def add(x, y):
    return x[0] + y[0], x[1] + y[1]


def sub(x, y):
    return x[0] - y[0], x[1] - y[1]


def turn(x):
    return -x[1], x[0]


def scale(x, numer, denom):
    numer %= denom
    if numer == 0:
        return x
    if 4 * numer == denom:
        return turn(x)
    if 2 * numer == denom:
        return -x[0], -x[1]
    if 4 * numer == 3 * denom:
        return x[1], -x[0]
    cosine = float(np.cos(2 * np.pi * numer / denom))
    sine = float(np.sin(2 * np.pi * numer / denom))
    return x[0] * cosine - x[1] * sine, x[0] * sine + x[1] * cosine


def dft4(x0, x1, x2, x3):
    even_sum, even_diff = add(x0, x2), sub(x0, x2)
    odd_sum, odd_diff = add(x1, x3), turn(sub(x1, x3))
    return (
        add(even_sum, odd_sum),
        add(even_diff, odd_diff),
        sub(even_sum, odd_sum),
        sub(even_diff, odd_diff),
    )


def dft16(items):
    firsts = [dft4(*[items[4 * j1 + j2] for j1 in range(4)]) for j2 in range(4)]
    result = [None] * 16
    for b1 in range(4):
        lasts = dft4(*[scale(firsts[j2][b1], j2 * b1, 16) for j2 in range(4)])
        for b2 in range(4):
            result[b1 + 4 * b2] = lasts[b2]
    return result


def row_kernel(
    x_ref, dft_hi_ref, cos_ref, sin_ref, out_ref, mid_ref, hi_ref, lo_ref, put_ref
):
    for half in range(2):
        rows = pl.ds(16 * half, 16)
        for kappa in range(4):
            lanes = pl.ds(128 * kappa, 128)
            items = [
                (x_ref[j, 0, rows, lanes].astype(F32), x_ref[j, 1, rows, lanes].astype(F32))
                for j in range(16)
            ]
            for a1, item in enumerate(dft16(items)):
                item = scale(item, kappa * a1, 64)
                mid_ref[kappa, a1, 0, rows, :] = item[0]
                mid_ref[kappa, a1, 1, rows, :] = item[1]
    for a1 in range(16):
        items = [(mid_ref[kappa, a1, 0], mid_ref[kappa, a1, 1]) for kappa in range(4)]
        for a2, item in enumerate(dft4(*items)):
            a = a1 + 16 * a2
            cosine = cos_ref[a : a + 1, :]
            sine = sin_ref[a : a + 1, :]
            real = item[0] * cosine - item[1] * sine
            imag = item[0] * sine + item[1] * cosine
            both = jnp.concatenate([real, imag], axis=1)
            high, low = split_value(both)
            hi_ref[a * 32 : (a + 1) * 32, :] = high
            lo_ref[a * 32 : (a + 1) * 32, :] = low
    dft_hi = dft_hi_ref[...]
    for n in range(8):
        high = hi_ref[n * 256 : (n + 1) * 256, :]
        low = lo_ref[n * 256 : (n + 1) * 256, :]
        made = nt_dot(dft_hi, high) + nt_dot(dft_hi, low)
        for part in range(2):
            for piece in range(2):
                half, i = divmod(2 * n + piece, 8)
                put_ref[pl.ds(half * 16 + part * 8 + i, 128, stride=PAD), :] = made[
                    part * 128 : (part + 1) * 128, piece * 128 : (piece + 1) * 128
                ]
    chunks = put_ref[...].reshape(128, PAD, 128)[:, :32]
    out_ref[...] = chunks.reshape(256, 16, 128).astype(BF16)


def row_transform(x):
    tables = [jnp.asarray(t) for t in row_tables()]
    return pl.pallas_call(
        row_kernel,
        out_shape=jax.ShapeDtypeStruct((256, 16, 128), BF16),
        in_specs=[LOCAL] * (1 + len(tables)),
        out_specs=LOCAL,
        scratch_shapes=[
            pltpu.VMEM((4, 16, 2, 32, 128), F32),
            pltpu.VMEM((2048, 256), BF16),
            pltpu.VMEM((2048, 256), BF16),
            pltpu.VMEM((128 * PAD, 128), F32),
        ],
        compiler_params=pltpu.CompilerParams(vmem_limit_bytes=VMEM_LIMIT),
        name="row_transform",
    )(x, *tables)


def column_kernel(
    x_ref, cos_ref, sin_ref, last_hi_ref, out_ref, mid_ref, real_ref, imag_ref, put_ref
):
    for chunk in range(16):
        items = []
        for band in range(16):
            value = x_ref[chunk * 16 + band].astype(F32)
            items.append((value[:8], value[8:]))
        for first, item in enumerate(dft16(items)):
            item = scale(item, first * chunk, 256)
            mid_ref[first, chunk, 0] = item[0]
            mid_ref[first, chunk, 1] = item[1]
    for first in range(16):
        items = [(mid_ref[first, chunk, 0], mid_ref[first, chunk, 1]) for chunk in range(16)]
        for second, item in enumerate(dft16(items)):
            at = first + 16 * second
            cosine = cos_ref[at : at + 1, :]
            sine = sin_ref[at : at + 1, :]
            rows = pl.ds(at, 8, stride=GAP)
            real_ref[rows, :] = item[0] * cosine - item[1] * sine
            imag_ref[rows, :] = item[0] * sine + item[1] * cosine
    last_hi = last_hi_ref[...]
    for g in range(8):
        both = jnp.concatenate(
            [real_ref[g * GAP : g * GAP + 256, :], imag_ref[g * GAP : g * GAP + 256, :]], axis=1
        )
        high, low = split_value(both)
        made = nt_dot(last_hi, high) + nt_dot(last_hi, low)
        for side in range(2):
            for m in range(4):
                start = (side * 32 + 4 * g + m) * PAD
                put_ref[start : start + 32, :] = made[
                    32 * m : 32 * m + 32, side * 128 : (side + 1) * 128
                ]
    for gamma in range(32):
        for side in range(2):
            start = gamma * 256 + side * 128
            out_ref[:, start : start + 128] = put_ref[
                pl.ds(side * 32 * PAD + gamma, 32, stride=PAD), :
            ]


def column_transform(x):
    tables = [jnp.asarray(t) for t in column_tables()]
    return pl.pallas_call(
        column_kernel,
        out_shape=jax.ShapeDtypeStruct((32, N), F32),
        in_specs=[LOCAL] * (1 + len(tables)),
        out_specs=LOCAL,
        scratch_shapes=[
            pltpu.VMEM((16, 16, 2, 8, 128), F32),
            pltpu.VMEM((8 * GAP, 128), F32),
            pltpu.VMEM((8 * GAP, 128), F32),
            pltpu.VMEM((64 * PAD, 128), F32),
        ],
        compiler_params=pltpu.CompilerParams(vmem_limit_bytes=VMEM_LIMIT),
        name="column_transform",
    )(x, *tables)


def block_of(index):
    row = index // SIDE
    col = index % SIDE
    return row // BAND, col // BAND, row % BAND * BAND + col % BAND


def send_code(own_row):
    band, column, slot = block_of(own_row)
    key = column * 16 + band
    number = jnp.arange(own_row.shape[0], dtype=jnp.int32)
    same = (key[None, :] == key[:, None]) & (number[:, None] < number[None, :])
    rank = jnp.sum(same.astype(jnp.int32), axis=0)
    return (key * CAP + rank)[None, :]


def receive_table(sub_index, my_band, my_column):
    band, column, slot = block_of(sub_index)
    inside = (band == my_band) & (column == my_column)
    count = sub_index.shape[1]
    before = (
        jnp.arange(count)[:, None] < jnp.arange(count)[None, :]
    ).astype(BF16)
    rank = jnp.dot(inside.astype(BF16), before, preferred_element_type=F32)
    hit = inside[:, None, :] & (rank[:, None, :] == jnp.arange(CAP, dtype=F32)[None, :, None])
    filled = jnp.any(hit, axis=2).reshape(-1)
    slots = jnp.sum(jnp.where(hit, slot[:, None, :], 0), axis=2).reshape(-1)
    entries = filled.shape[0]
    number = jnp.arange(entries, dtype=jnp.int32)
    place = jnp.sum(
        ((number[None, :] < number[:, None]) & filled[None, :]).astype(jnp.int32), axis=1
    )
    chosen = filled[None, :] & (place[None, :] == number[:, None])
    order = jnp.sum(jnp.where(chosen, number[None, :], 0), axis=1)
    sorted_slots = jnp.sum(jnp.where(chosen, slots[None, :], 0), axis=1)
    total = jnp.sum(filled.astype(jnp.int32)).reshape(1)
    return order, sorted_slots, total


def shards(visibilities, coordinates, phases, sub_index):
    facet_id = lax.axis_index("facet")
    span_id = lax.axis_index("span")
    with jax.named_scope("rotate"):
        parts = rotate_blocks(visibilities[0], coordinates[0], phases[0])
    with jax.named_scope("spread_span"):
        spread = lax.all_to_all(parts, "facet", split_axis=0, concat_axis=0, tiled=True)
    with jax.named_scope("choose"):
        own_row = lax.dynamic_index_in_dim(sub_index, span_id, 0, keepdims=False)
        order, slots, count = receive_table(sub_index, span_id, facet_id)
        spread, order, slots, count = lax.optimization_barrier((spread, order, slots, count))
        chosen = pick_blocks(send_code(own_row), spread.reshape(-1, 256))
    with jax.named_scope("to_owner"):
        arrived = lax.all_to_all(
            chosen, ("facet", "span"), split_axis=0, concat_axis=0, tiled=True
        )
    with jax.named_scope("gridding"):
        block = grid_blocks(order, slots, count, arrived)
    with jax.named_scope("to_rows"):
        rows = lax.all_to_all(block, "facet", split_axis=0, concat_axis=0, tiled=True)
    with jax.named_scope("rows_dft"):
        half_done = row_transform(rows)
    with jax.named_scope("to_columns"):
        columns = lax.all_to_all(
            half_done, ("facet", "span"), split_axis=0, concat_axis=0, tiled=True
        )
    with jax.named_scope("columns_dft"):
        return column_transform(columns)


def solution(mesh):
    return jax.shard_map(
        shards,
        mesh=mesh,
        in_specs=(
            P("span", "facet", None, None),
            P("span", "facet", None, None),
            P("span", "facet", None),
            P(),
        ),
        out_specs=P(("facet", "span"), None),
        check_vma=False,
    )
```
